512 devices in a mesh: row: 32 (over z, core), col: 16 (over x, y).
Axes of the slice: x: 4, y: 4, z: 16, core: 2. Of those that a mesh axis runs over, the one named last changes fastest.
Arguments:
- slab: float32 [16384, 4096], P('row', 'col'), may hold values from -6 to 6
- panels: float32 [3, 16384, 512], P(None, 'row', 'col'), may hold values from -0.125 to 0.125
- pivots: int32 [3, 512], replicated, may hold values from 0 to 16383, as said below
Outputs:
- updated_slab: float32 [16384, 4096], P('row', 'col')
The draws below stay inside these ranges and needn't reach their ends.
Inputs may be any that keep to these rules, and one draw needn't show every extreme that they name: Each pivots[k, i] is either k * 512 + i or a row at or below (k + 1) * 512; the rows of one panel are distinct.
All inputs are finite; a program needn't handle non-finite values.
Results may differ from the reference program's by a relative error of at most 0.0001.
Values sent between devices are 32-bit elements; how exact they have to be, the bound alone decides.
A program may use at most 64 MiB of HBM per device.

```python
import jax
import jax.numpy as jnp
from jax import lax

NB = 512
TICKS = 3
M = 16384
N = 4096


def draw_pivots(key, part):
    lists = []
    for tick in range(TICKS):
        sub = jax.random.fold_in(key, 7 + tick)
        start = tick * NB
        order = jax.random.permutation(jax.random.fold_in(sub, 1), M - start - NB).astype(jnp.int32)
        lowest = jnp.argmin(order).astype(jnp.int32)
        order = order.at[lowest].set(order[NB - 1]).at[NB - 1].set(0)
        lower_rows = (M - 1 - order[:NB]).astype(jnp.int32)
        flips = jax.random.randint(jax.random.fold_in(sub, 2), (NB,), 0, 2)
        flips = flips.at[0].set(0).at[NB - 1].set(1)
        stay = start + jnp.arange(NB, dtype=jnp.int32)
        lists.append(jnp.where(flips == 1, lower_rows, stay).astype(jnp.int32))
    return jnp.stack(lists)


def block_scale(stream_key, dims, cuts, smallest, high):
    factor_of, own = 1.0, jax.random.fold_in(stream_key, 6)
    for position, blocks in cuts:
        heights = jnp.exp(jax.random.uniform(jax.random.fold_in(own, position), (blocks,), jnp.float32, smallest / len(cuts), high / len(cuts)))
        factor_of = factor_of * jnp.repeat(heights, dims[position] // blocks).reshape([-1 if axis == position else 1 for axis in range(len(dims))])
    return factor_of


def normal_values(own_key, shape, scale, bound, cuts=(), kind=jnp.bfloat16):
    gain = block_scale(own_key, shape, cuts, -0.22, 0.18) if cuts else 1.0
    values = jax.random.normal(own_key, shape, jnp.float32) * scale * gain
    return jnp.minimum(jnp.maximum(values, -bound), bound).astype(kind)


def setup_inputs(seed: int = 0) -> dict:
    keys = jax.random.split(jax.random.key(seed), 4)
    slab = normal_values(keys[0], (M, N), 1.0, 6.0, ((0, 32), (1, 16)), jnp.float32)
    panels = normal_values(keys[1], (TICKS, M, NB), (4 * NB) ** -0.5, 0.125, ((1, 32), (2, 16)), jnp.float32)
    pivots = draw_pivots(jax.random.fold_in(keys[3], 71), 0)
    return {"slab": slab, "panels": panels, "pivots": pivots}


def reference(slab, panels, pivots):
    matrix = slab
    for tick in range(TICKS):
        start = tick * NB
        sources = pivots[tick]
        old_top = matrix[start:start + NB]
        new_top = matrix[sources]
        matrix = matrix.at[sources].set(old_top)
        unit_lower = jnp.tril(panels[tick, start:start + NB], -1) + jnp.eye(NB, dtype=jnp.float32)
        upper = lax.linalg.triangular_solve(unit_lower, new_top, left_side=True, lower=True, unit_diagonal=True)
        matrix = matrix.at[start:start + NB].set(upper)
        below = matrix[start + NB:] - jnp.dot(panels[tick, start + NB:].astype(jnp.float32), upper.astype(jnp.float32), precision=lax.Precision.HIGHEST, preferred_element_type=jnp.float32)
        matrix = matrix.at[start + NB:].set(below)
    return matrix
```

```python
import functools

import jax
import jax.numpy as jnp
from jax import lax
from jax.experimental import pallas as pl
from jax.experimental.pallas import tpu as pltpu
from jax.sharding import PartitionSpec as P

MESH = pl.DeviceIdType.MESH
HIGHEST = lax.Precision.HIGHEST
SIDE = 4
SLOTS = 64
CHUNKS = 16
LAG = 2
TILE = 128


def contract(a, b):
    return lax.dot_general(
        a, b, (((0,), (0,)), ((), ())), precision=HIGHEST, preferred_element_type=jnp.float32
    )


def exchange_kernel(tops, z_size, top_ref, piece_ref, x_ref, g_ref, xo_ref, *sems):
    (zp_s, zp_r, zm_s, zm_r, pr_s, pr_r, b_r, bp_s, bm_s, bc_s, x_s, x_r, loc) = sems
    row, col = lax.axis_index("row"), lax.axis_index("col")
    z, core = row // 2, row % 2
    xx, yy = col // SIDE, col % SIDE
    up = (2 * ((z + 1) % z_size) + core, col)
    down = (2 * ((z + z_size - 1) % z_size) + core, col)
    partner = (2 * z + 1 - core, col)

    def side(step_x, step_y):
        return (row, ((xx + step_x) % SIDE) * SIDE + (yy + step_y) % SIDE)

    barrier = pltpu.get_barrier_semaphore()
    near = (up, down, partner, side(1, 0), side(SIDE - 1, 0), side(0, 1), side(0, SIDE - 1))
    for device in near:
        pl.semaphore_signal(barrier, inc=1, device_id=device, device_id_type=MESH)
    pl.semaphore_wait(barrier, len(near))

    count, height = piece_ref.shape[0], top_ref.shape[0]
    base = tops * height
    chunk = height // CHUNKS

    def remote(src, dst, send, recv, device):
        return pltpu.make_async_remote_copy(
            src_ref=src, dst_ref=dst, send_sem=send, recv_sem=recv, device_id=device, device_id_type=MESH
        )

    def slot(origin_z):
        return g_ref.at[pl.ds(pl.multiple_of(base + (2 * origin_z + core) * count, 8), count), :]

    my_piece = pltpu.make_async_copy(piece_ref, slot(z), loc.at[0])
    my_x = pltpu.make_async_copy(x_ref, xo_ref.at[col], loc.at[1])
    my_piece.start()
    my_x.start()

    ups, downs = z_size // 2, z_size - 1 - z_size // 2

    def send_up(s):
        ref = slot((z + z_size - s) % z_size)
        return remote(ref, ref, zp_s.at[s], zp_r.at[s], up)

    def send_down(s):
        ref = slot((z + s) % z_size)
        return remote(ref, ref, zm_s.at[s], zm_r.at[s], down)

    def got_up(s):
        ref = slot((z + 2 * z_size - 1 - s) % z_size)
        return remote(ref, ref, zp_s.at[s], zp_r.at[s], up)

    def got_down(s):
        ref = slot((z + 1 + s) % z_size)
        return remote(ref, ref, zm_s.at[s], zm_r.at[s], down)

    def share(hops):
        ref = slot((z + z_size - hops) % z_size)
        return remote(ref, ref, pr_s.at[hops], pr_r.at[hops], partner)

    def ring_step(s):
        @pl.when(s <= ups)
        def _():
            got_up(s - 1).wait_recv()

            @pl.when(s < ups)
            def _():
                send_up(s).start()

            share(s).start()

        @pl.when(s <= downs)
        def _():
            got_down(s - 1).wait_recv()

            @pl.when(s < downs)
            def _():
                send_down(s).start()

            share(z_size - s).start()

    def top_rows(b, i):
        return g_ref.at[pl.ds(pl.multiple_of(b * height + i * chunk, 8), chunk), :]

    def hops_of(b):
        h = (z + z_size - b // 2) % z_size
        return h, jnp.where(h <= ups, h, z_size - h)

    def top_copy(b, i, kind):
        ref = top_rows(b, i)
        send, device = {"up": (bp_s, up), "down": (bm_s, down), "core": (bc_s, partner)}[kind]
        return remote(ref, ref, send.at[b, i], b_r.at[b, i], device)

    def top_roles(b):
        h, hops = hops_of(b)
        mine = core == b % 2
        return mine, mine & (h < ups), mine & ((h == 0) | (h > ups + 1)), mine & (h > 0), hops

    def top_step(t):
        for b in range(tops):
            mine, to_up, to_down, gets, hops = top_roles(b)
            i = t - LAG * hops
            inside = (i >= 0) & (i < CHUNKS)

            @pl.when(inside & gets)
            def _():
                top_copy(b, i, "up").wait_recv()

            @pl.when(inside & to_up)
            def _():
                top_copy(b, i, "up").start()

            @pl.when(inside & to_down)
            def _():
                top_copy(b, i, "down").start()

            @pl.when(inside & mine)
            def _():
                top_copy(b, i, "core").start()

    rows = x_ref.shape[0]
    half, quarter = rows // 2, rows // 4

    def x_piece(k, first, second, part):
        a = (xx if k == 0 else yy) + first
        b = (yy if k == 0 else xx) + second
        a, b = a % SIDE, b % SIDE
        c = a * SIDE + b if k == 0 else b * SIDE + a
        start, size = {"all": (0, half), "low": (0, quarter), "high": (quarter, quarter)}[part]
        return xo_ref.at[c, pl.ds(k * half + start, size), :]

    def x_send(k, stage, v, e, receive=False):
        first = (0, SIDE - 1, 1, 2)[v]
        move = {0: (0, "all"), 1: (0, "all"), 2: (SIDE - 1, "low"), 3: (1, "high")}[e]
        step = 1 if e in (0, 2) else SIDE - 1
        along_x = (k == 0) == (stage == 0)
        device = side(step, 0) if along_x else side(0, step)
        n = (k * 5 + (0 if stage == 0 else 1 + v)) * 4 + e
        back = {0: (SIDE - 1, "all"), 1: (1, "all"), 2: (2, "low"), 3: (2, "high")}[e]
        if stage == 0:
            src, dst = x_piece(k, move[0], 0, move[1]), x_piece(k, back[0], 0, back[1])
        else:
            src, dst = x_piece(k, first, move[0], move[1]), x_piece(k, first, back[0], back[1])
        if e < 2 and (stage == 0 or v == 0):
            src_send = x_ref.at[pl.ds(k * half, half), :]
        else:
            src_send = src
        if receive:
            return remote(dst, dst, x_s.at[n], x_r.at[n], device)
        return remote(src_send, src, x_s.at[n], x_r.at[n], device)

    def start(stage, v, e):
        for k in range(2):
            x_send(k, stage, v, e).start()

    def arrive(stage, v, e):
        for k in range(2):
            x_send(k, stage, v, e, True).wait_recv()

    def pair(stage, v, fns):
        for e in fns:
            start(stage, v, e)

    def pass_on(stage, v):
        arrive(stage, v, 0)
        start(stage, v, 2)
        arrive(stage, v, 1)
        start(stage, v, 3)

    def x_event(number):
        if number == 0:
            arrive(0, 0, 0)
            start(0, 0, 2)
            pair(1, 1, (0, 1))
            arrive(0, 0, 1)
            start(0, 0, 3)
            pair(1, 2, (0, 1))
        elif number == 1:
            pass_on(1, 0)
        elif number == 2:
            arrive(0, 0, 2)
            arrive(0, 0, 3)
            pair(1, 3, (0, 1))
        elif number == 3:
            pass_on(1, 1)
        elif number == 4:
            pass_on(1, 2)
        elif number == 5:
            pass_on(1, 3)

    pair(0, 0, (0, 1))
    pair(1, 0, (0, 1))
    my_piece.wait()
    send_up(0).start()
    send_down(0).start()
    share(0).start()
    if tops:
        for b in range(tops):
            @pl.when(row == b)
            def _():
                own = pltpu.make_async_copy(top_ref, g_ref.at[pl.ds(b * height, height), :], loc.at[2])
                own.start()
                own.wait()
    my_x.wait()

    total = LAG * ups + (CHUNKS if tops else 1)
    marks = [2 + (total - 2) * m // 6 for m in range(6)] + [total]
    begin = 0
    for number, end in enumerate(marks):
        def step(t, carry):
            if tops:
                top_step(t)
            s = t // LAG

            @pl.when((t % LAG == 0) & (s >= 1))
            def _():
                ring_step(s)

            return carry

        lax.fori_loop(begin, end, step, 0)
        begin = end
        x_event(number)

    for v in range(4):
        arrive(1, v, 2)
        arrive(1, v, 3)

    def drain_up(s, carry):
        send_up(s).wait_send()
        return carry

    def drain_down(s, carry):
        send_down(s).wait_send()
        return carry

    def drain_share(s, carry):
        share(s).wait_send()
        ref = slot((z + z_size - s) % z_size)
        other = g_ref.at[pl.ds(pl.multiple_of(base + (2 * ((z + z_size - s) % z_size) + 1 - core) * count, 8), count), :]
        remote(ref, other, pr_s.at[s], pr_r.at[s], partner).wait_recv()
        return carry

    lax.fori_loop(0, ups, drain_up, 0)
    lax.fori_loop(0, downs, drain_down, 0)
    lax.fori_loop(0, z_size, drain_share, 0)
    if tops:
        def drain_top(i, carry):
            for b in range(tops):
                mine, to_up, to_down, gets, hops = top_roles(b)

                @pl.when(jnp.logical_not(mine))
                def _():
                    top_copy(b, i, "core").wait_recv()

                @pl.when(to_up)
                def _():
                    top_copy(b, i, "up").wait_send()

                @pl.when(to_down)
                def _():
                    top_copy(b, i, "down").wait_send()

                @pl.when(mine)
                def _():
                    top_copy(b, i, "core").wait_send()

            return carry

        lax.fori_loop(0, CHUNKS, drain_top, 0)
    for k in range(2):
        for e in range(4):
            x_send(k, 0, 0, e).wait_send()
        for v in range(4):
            for e in range(4):
                x_send(k, 1, v, e).wait_send()


def exchange(top, piece, x, tops, owners, ident):
    height, width = top.shape
    count = piece.shape[0]
    z_size = owners // 2
    dma = pltpu.SemaphoreType.DMA
    vmem = pl.BlockSpec(memory_space=pltpu.VMEM)
    hbm = pl.BlockSpec(memory_space=pl.ANY)
    blocks = max(tops, 1)
    g, xo = pl.pallas_call(
        functools.partial(exchange_kernel, tops, z_size),
        out_shape=(
            jax.ShapeDtypeStruct((tops * height + owners * count, width), jnp.float32),
            jax.ShapeDtypeStruct((SIDE * SIDE,) + x.shape, jnp.float32),
        ),
        in_specs=[vmem, vmem, vmem],
        out_specs=(hbm, hbm),
        scratch_shapes=[
            dma((z_size,)), dma((z_size,)), dma((z_size,)), dma((z_size,)),
            dma((z_size,)), dma((z_size,)),
            dma((blocks, CHUNKS)), dma((blocks, CHUNKS)), dma((blocks, CHUNKS)), dma((blocks, CHUNKS)),
            dma((40,)), dma((40,)), dma((3,)),
        ],
        compiler_params=pltpu.CompilerParams(collective_id=ident, has_side_effects=True),
    )(top, piece, x)
    return g, xo.reshape(SIDE * SIDE * x.shape[0], x.shape[1])


def invert_tile(tile):
    k = lax.broadcasted_iota(jnp.int32, tile.shape, 0)
    r = lax.broadcasted_iota(jnp.int32, tile.shape, 1)
    mul = functools.partial(jnp.dot, precision=HIGHEST, preferred_element_type=jnp.float32)
    eye = jnp.where(k == r, 1.0, 0.0).astype(jnp.float32)
    strict = jnp.where(k < r, tile, 0.0)
    power = jnp.where(k // 16 == r // 16, -strict, 0.0)
    inverse = eye + power
    for _ in range(3):
        power = mul(power, power)
        inverse = inverse + mul(inverse, power)
    for size in (16, 32, 64):
        off = jnp.where((k // (2 * size) == r // (2 * size)) & (k // size != r // size), strict, 0.0)
        inverse = inverse - mul(inverse, mul(off, inverse))
    return inverse


def solve_kernel(ticks, width, x_ref, t_ref, u_ref, inverse_ref):
    tiles = width // TILE

    def invert(n, carry):
        b, j = n // tiles, n % tiles
        across = pl.ds(pl.multiple_of(n * TILE, TILE), TILE)
        inverse_ref[across, :] = invert_tile(x_ref[pl.ds(pl.multiple_of(j * TILE, TILE), TILE), across])
        return carry

    lax.fori_loop(0, ticks * tiles, invert, 0)
    off = ticks * width
    for b in range(ticks):
        rhs = t_ref[pl.ds(b * width, width), :]
        for j in range(b):
            block = x_ref[:, pl.ds(off, width)]
            off += width
            rhs = rhs - contract(block, u_ref[pl.ds(j * width, width), :])
        for j in range(tiles):
            here = b * width + j * TILE
            part = rhs[j * TILE:(j + 1) * TILE]
            if j:
                part = part - contract(
                    x_ref[pl.ds(0, j * TILE), pl.ds(here, TILE)], u_ref[pl.ds(b * width, j * TILE), :]
                )
            u_ref[pl.ds(here, TILE), :] = contract(inverse_ref[pl.ds(here, TILE), :], part)


def solve(x, t, ticks, width):
    vmem = pl.BlockSpec(memory_space=pltpu.VMEM)
    return pl.pallas_call(
        functools.partial(solve_kernel, ticks, width),
        out_shape=jax.ShapeDtypeStruct(t.shape, jnp.float32),
        in_specs=[vmem, vmem],
        out_specs=vmem,
        scratch_shapes=[pltpu.VMEM((ticks * width, TILE), jnp.float32)],
        compiler_params=pltpu.CompilerParams(vmem_limit_bytes=50 * 1024 * 1024),
    )(x, t)


def find(a, b, base):
    i = jnp.arange(b.shape[0], dtype=jnp.int32)
    return jnp.max(jnp.where(a[:, None] == b[None, :], base + i[None, :], -1), axis=1)


def packing(pivots, rows):
    src = pivots.reshape(-1)
    owner = src // rows
    e = jnp.arange(src.shape[0], dtype=jnp.int32)
    same = (owner[:, None] == owner[None, :]) & (e[None, :] < e[:, None])
    return src, owner, jnp.sum(same.astype(jnp.int32), axis=1)


def update(packed, owners, slab, panels, pivots):
    rows, cols = slab.shape
    ticks, width = pivots.shape
    depth = panels.shape[2]
    me = lax.axis_index("row")
    src, owner, rank = packing(pivots, rows)
    top = ticks * width
    ident = 0 if packed else 2
    panel_rows = jnp.concatenate(
        [panels[k] for k in range(ticks)] + [jnp.zeros((rows, 128 - ticks * depth), jnp.float32)], axis=1
    )
    if packed:
        count, tops, patch = SLOTS, ticks, 128
        g = jnp.where(owner < ticks, src, top + owner * count + rank)
        s = jnp.arange(count, dtype=jnp.int32)
        held = (owner[None, :] == me) & (rank[None, :] == s[:, None])
        listed = jnp.max(jnp.where(held, src[None, :] - me * rows, 0), axis=1)
        panel_piece = jnp.take(panel_rows, listed, axis=0)
        slab_piece = jnp.take(slab, listed, axis=0)
    else:
        count, tops, patch = rows, 0, rows
        g = src
        panel_piece, slab_piece = panel_rows, slab

    x_panels = jnp.transpose(panels, (2, 0, 1)).reshape(depth, ticks * rows)
    g_panel, full = exchange(panel_rows, panel_piece, x_panels, tops, owners, ident)

    s0, s1, s2 = pivots
    g0, g1, g2 = g[:width], g[width:2 * width], g[2 * width:]
    back = find(s2, s1, width)
    f2 = find(jnp.where(back >= 0, back, s2), s0, 0)
    f1 = find(s1, s0, 0)
    row20 = jnp.where(back >= 0, back, g2)
    take_t = jnp.concatenate([g0, jnp.where(f1 >= 0, f1, g1), jnp.where(f2 >= 0, f2, row20)])
    mine = me * rows + jnp.arange(rows, dtype=jnp.int32)
    h2 = find(mine, s2, 2 * width)
    pos1 = jnp.where(h2 >= 0, h2, mine)
    h1 = find(pos1, s1, width)
    pos0 = jnp.where(h1 >= 0, h1, pos1)
    h0 = find(pos0, s0, 0)
    orig = jnp.where(h0 >= 0, h0, pos0)
    moved0, moved1 = pos0 != mine, pos1 != mine
    if packed:
        touched = orig != mine
        q = jnp.arange(rows, dtype=jnp.int32)
        place = jnp.sum(((q[None, :] < q[:, None]) & touched[None, :]).astype(jnp.int32), axis=1)
        s = jnp.arange(patch, dtype=jnp.int32)
        pick = (place[None, :] == s[:, None]) & touched[None, :]
        from0 = jnp.max(jnp.where(pick & moved0[None, :], pos0[None, :], 0), axis=1)
        from1 = jnp.max(jnp.where(pick & moved1[None, :], pos1[None, :], 0), axis=1)
    else:
        from0, from1 = pos0, pos1
    corner = jnp.concatenate([
        g_panel[:width, 0:depth],
        g_panel[width:2 * width, depth:2 * depth],
        g_panel[2 * width:3 * width, 2 * depth:3 * depth],
        jnp.take(g_panel, g1, axis=0)[:, 0:depth],
        jnp.take(g_panel, row20, axis=0)[:, 0:depth],
        jnp.take(g_panel, g2, axis=0)[:, depth:2 * depth],
        jnp.take(g_panel, from0, axis=0)[:, 0:depth],
        jnp.take(g_panel, from1, axis=0)[:, depth:2 * depth],
    ]).T
    g_slab, factor = exchange(slab, slab_piece, corner, tops, owners, ident + 1)

    t = jnp.take(g_slab, take_t, axis=0)
    kept = jnp.take(g_slab, jnp.where(orig != mine, orig, 0), axis=0)
    base = jnp.where((orig != mine)[:, None], kept, slab)
    left = []
    for k, moved in ((0, moved0), (1, moved1)):
        new = factor[:, 2 * top + k * patch:2 * top + (k + 1) * patch]
        if packed:
            new = jnp.dot(new, pick.astype(jnp.float32), precision=HIGHEST, preferred_element_type=jnp.float32)
        left.append(jnp.where(moved[None, :], new, full[:, k * rows:(k + 1) * rows]))
    left.append(full[:, 2 * rows:3 * rows])
    return factor[:, :2 * top + 2 * 128], t, base, left


def solution(mesh):
    owners = mesh.shape["row"]

    def local(slab, panels, pivots):
        rows, ticks = slab.shape[0], pivots.shape[0]
        _, owner, rank = packing(pivots, rows)
        fits = jnp.all((owner < ticks) | (rank < SLOTS))
        factor, t, base, left = lax.cond(
            fits,
            functools.partial(update, True, owners),
            functools.partial(update, False, owners),
            slab, panels, pivots,
        )
        width = pivots.shape[1]
        upper = solve(factor, t, ticks, width)
        me = lax.axis_index("row")
        lowered = base
        for k in range(ticks):
            lowered = lowered - contract(left[k], upper[k * width:(k + 1) * width])
        for k in range(ticks):
            lowered = jnp.where(me == k, upper[k * width:(k + 1) * width], lowered)
        return lowered

    in_specs = (P("row", "col"), P(None, "row", "col"), P())
    return jax.shard_map(local, mesh=mesh, in_specs=in_specs, out_specs=P("row", "col"), check_vma=False)
```

```python
import functools

import jax
import jax.numpy as jnp
from jax import lax
from jax.experimental import pallas as pl
from jax.experimental.pallas import tpu as pltpu
from jax.sharding import PartitionSpec as P

MESH = pl.DeviceIdType.MESH
SIDE = 4
SLOTS = 64
CHUNKS = 8
LAG = 4
TILE = 128
PATCH = 128


def split(a):
    high = a.astype(jnp.bfloat16)
    return high, (a - high.astype(jnp.float32)).astype(jnp.bfloat16)


def mul(a, b):
    dot = functools.partial(jnp.dot, preferred_element_type=jnp.float32)
    (ah, al), (bh, bl) = split(a), split(b)
    return dot(ah, bh) + (dot(ah, bl) + dot(al, bh))


def exchange_kernel(tops, z_size, LAG, CHUNKS, top_ref, piece_ref, x_ref, g_ref, xo_ref, *sems):
    (zp_s, zp_r, zm_s, zm_r, pr_s, pr_r, b_r, bp_s, bm_s, bc_s, x_s, x_r, loc) = sems
    row, col = lax.axis_index("row"), lax.axis_index("col")
    z, core = row // 2, row % 2
    xx, yy = col // SIDE, col % SIDE
    up = (2 * ((z + 1) % z_size) + core, col)
    down = (2 * ((z + z_size - 1) % z_size) + core, col)
    partner = (2 * z + 1 - core, col)

    def side(step_x, step_y):
        return (row, ((xx + step_x) % SIDE) * SIDE + (yy + step_y) % SIDE)

    barrier = pltpu.get_barrier_semaphore()
    near = (up, down, partner, side(1, 0), side(SIDE - 1, 0), side(0, 1), side(0, SIDE - 1))
    for device in near:
        pl.semaphore_signal(barrier, inc=1, device_id=device, device_id_type=MESH)
    pl.semaphore_wait(barrier, len(near))

    count, height = piece_ref.shape[0], top_ref.shape[0]
    base = tops * height
    chunk = height // CHUNKS

    def remote(src, dst, send, recv, device):
        return pltpu.make_async_remote_copy(
            src_ref=src, dst_ref=dst, send_sem=send, recv_sem=recv, device_id=device, device_id_type=MESH
        )

    def slot(origin_z):
        return g_ref.at[pl.ds(pl.multiple_of(base + (2 * origin_z + core) * count, 8), count), :]

    my_piece = pltpu.make_async_copy(piece_ref, slot(z), loc.at[0])
    my_x = pltpu.make_async_copy(x_ref, xo_ref.at[:, col], loc.at[1])
    my_piece.start()
    my_x.start()

    ups, downs = z_size // 2, z_size - 1 - z_size // 2

    def send_up(s):
        ref = slot((z + z_size - s) % z_size)
        return remote(ref, ref, zp_s.at[s], zp_r.at[s], up)

    def send_down(s):
        ref = slot((z + s) % z_size)
        return remote(ref, ref, zm_s.at[s], zm_r.at[s], down)

    def got_up(s):
        ref = slot((z + 2 * z_size - 1 - s) % z_size)
        return remote(ref, ref, zp_s.at[s], zp_r.at[s], up)

    def got_down(s):
        ref = slot((z + 1 + s) % z_size)
        return remote(ref, ref, zm_s.at[s], zm_r.at[s], down)

    def share(hops):
        ref = slot((z + z_size - hops) % z_size)
        return remote(ref, ref, pr_s.at[hops], pr_r.at[hops], partner)

    def ring_step(s):
        @pl.when(s <= ups)
        def _():
            got_up(s - 1).wait_recv()

            @pl.when(s < ups)
            def _():
                send_up(s).start()

            share(s).start()

        @pl.when(s <= downs)
        def _():
            got_down(s - 1).wait_recv()

            @pl.when(s < downs)
            def _():
                send_down(s).start()

            share(z_size - s).start()

    def top_rows(b, i):
        return g_ref.at[pl.ds(pl.multiple_of(b * height + i * chunk, 8), chunk), :]

    def hops_of(b):
        h = (z + z_size - b // 2) % z_size
        return h, jnp.where(h <= ups, h, z_size - h)

    def top_copy(b, i, kind):
        ref = top_rows(b, i)
        send, device = {"up": (bp_s, up), "down": (bm_s, down), "core": (bc_s, partner)}[kind]
        return remote(ref, ref, send.at[b, i], b_r.at[b, i], device)

    def top_roles(b):
        h, hops = hops_of(b)
        mine = core == b % 2
        return mine, mine & (h < ups), mine & ((h == 0) | (h > ups + 1)), mine & (h > 0), hops

    def top_step(t):
        for b in range(tops):
            mine, to_up, to_down, gets, hops = top_roles(b)
            i = t - LAG * hops
            inside = (i >= 0) & (i < CHUNKS)

            @pl.when(inside & gets)
            def _():
                top_copy(b, i, "up").wait_recv()

            @pl.when(inside & to_up)
            def _():
                top_copy(b, i, "up").start()

            @pl.when(inside & to_down)
            def _():
                top_copy(b, i, "down").start()

            @pl.when(inside & mine)
            def _():
                top_copy(b, i, "core").start()

    rows = x_ref.shape[1]
    half, quarter = rows // 2, rows // 4

    def x_piece(k, first, second, part):
        a = (xx if k == 0 else yy) + first
        b = (yy if k == 0 else xx) + second
        a, b = a % SIDE, b % SIDE
        c = a * SIDE + b if k == 0 else b * SIDE + a
        start, size = {"all": (0, half), "low": (0, quarter), "high": (quarter, quarter)}[part]
        return xo_ref.at[:, c, pl.ds(k * half + start, size), :]

    def x_send(k, stage, v, e, receive=False):
        first = (0, SIDE - 1, 1, 2)[v]
        move = {0: (0, "all"), 1: (0, "all"), 2: (SIDE - 1, "low"), 3: (1, "high")}[e]
        step = 1 if e in (0, 2) else SIDE - 1
        along_x = (k == 0) == (stage == 0)
        device = side(step, 0) if along_x else side(0, step)
        n = (k * 5 + (0 if stage == 0 else 1 + v)) * 4 + e
        back = {0: (SIDE - 1, "all"), 1: (1, "all"), 2: (2, "low"), 3: (2, "high")}[e]
        if stage == 0:
            src, dst = x_piece(k, move[0], 0, move[1]), x_piece(k, back[0], 0, back[1])
        else:
            src, dst = x_piece(k, first, move[0], move[1]), x_piece(k, first, back[0], back[1])
        if e < 2 and (stage == 0 or v == 0):
            src_send = x_ref.at[:, pl.ds(k * half, half), :]
        else:
            src_send = src
        if receive:
            return remote(dst, dst, x_s.at[n], x_r.at[n], device)
        return remote(src_send, src, x_s.at[n], x_r.at[n], device)

    def start(stage, v, e):
        for k in range(2):
            x_send(k, stage, v, e).start()

    def arrive(stage, v, e):
        for k in range(2):
            x_send(k, stage, v, e, True).wait_recv()

    def pair(stage, v, fns):
        for e in fns:
            start(stage, v, e)

    def pass_on(stage, v):
        arrive(stage, v, 0)
        start(stage, v, 2)
        arrive(stage, v, 1)
        start(stage, v, 3)

    def x_event(number):
        if number == 0:
            arrive(0, 0, 0)
            start(0, 0, 2)
            pair(1, 1, (0, 1))
            arrive(0, 0, 1)
            start(0, 0, 3)
            pair(1, 2, (0, 1))
        elif number == 1:
            pass_on(1, 0)
        elif number == 2:
            arrive(0, 0, 2)
            arrive(0, 0, 3)
            pair(1, 3, (0, 1))
        elif number == 3:
            pass_on(1, 1)
        elif number == 4:
            pass_on(1, 2)
        elif number == 5:
            pass_on(1, 3)

    pair(0, 0, (0, 1))
    pair(1, 0, (0, 1))
    my_piece.wait()
    send_up(0).start()
    send_down(0).start()
    share(0).start()
    if tops:
        for b in range(tops):
            @pl.when(row == b)
            def _():
                own = pltpu.make_async_copy(top_ref, g_ref.at[pl.ds(b * height, height), :], loc.at[2])
                own.start()
                own.wait()
    my_x.wait()

    total = LAG * ups + (CHUNKS if tops else 1)
    marks = [2 + (total - 2) * m // 6 for m in range(6)] + [total]
    begin = 0
    for number, end in enumerate(marks):
        def step(t, carry):
            if tops:
                top_step(t)
            s = t // LAG

            @pl.when((t % LAG == 0) & (s >= 1))
            def _():
                ring_step(s)

            return carry

        lax.fori_loop(begin, end, step, 0)
        begin = end
        x_event(number)

    for v in range(4):
        arrive(1, v, 2)
        arrive(1, v, 3)

    def drain_up(s, carry):
        send_up(s).wait_send()
        return carry

    def drain_down(s, carry):
        send_down(s).wait_send()
        return carry

    def drain_share(s, carry):
        share(s).wait_send()
        ref = slot((z + z_size - s) % z_size)
        other = g_ref.at[pl.ds(pl.multiple_of(base + (2 * ((z + z_size - s) % z_size) + 1 - core) * count, 8), count), :]
        remote(ref, other, pr_s.at[s], pr_r.at[s], partner).wait_recv()
        return carry

    lax.fori_loop(0, ups, drain_up, 0)
    lax.fori_loop(0, downs, drain_down, 0)
    lax.fori_loop(0, z_size, drain_share, 0)
    if tops:
        def drain_top(i, carry):
            for b in range(tops):
                mine, to_up, to_down, gets, hops = top_roles(b)

                @pl.when(jnp.logical_not(mine))
                def _():
                    top_copy(b, i, "core").wait_recv()

                @pl.when(to_up)
                def _():
                    top_copy(b, i, "up").wait_send()

                @pl.when(to_down)
                def _():
                    top_copy(b, i, "down").wait_send()

                @pl.when(mine)
                def _():
                    top_copy(b, i, "core").wait_send()

            return carry

        lax.fori_loop(0, CHUNKS, drain_top, 0)
    for k in range(2):
        for e in range(4):
            x_send(k, 0, 0, e).wait_send()
        for v in range(4):
            for e in range(4):
                x_send(k, 1, v, e).wait_send()


def exchange(top, piece, x, tops, owners, ident, lag=LAG, chunks=CHUNKS, space=pl.ANY):
    height, width = top.shape
    count = piece.shape[0]
    z_size = owners // 2
    dma = pltpu.SemaphoreType.DMA
    vmem = pl.BlockSpec(memory_space=pltpu.VMEM)
    hbm = pl.BlockSpec(memory_space=space)
    blocks = max(tops, 1)
    g, xo = pl.pallas_call(
        functools.partial(exchange_kernel, tops, z_size, lag, chunks),
        out_shape=(
            jax.ShapeDtypeStruct((tops * height + owners * count, width), jnp.float32),
            jax.ShapeDtypeStruct((x.shape[0], SIDE * SIDE) + x.shape[1:], jnp.float32),
        ),
        in_specs=[vmem, vmem, vmem],
        out_specs=(hbm, hbm),
        scratch_shapes=[
            dma((z_size,)), dma((z_size,)), dma((z_size,)), dma((z_size,)),
            dma((z_size,)), dma((z_size,)),
            dma((blocks, chunks)), dma((blocks, chunks)), dma((blocks, chunks)), dma((blocks, chunks)),
            dma((40,)), dma((40,)), dma((3,)),
        ],
        compiler_params=pltpu.CompilerParams(collective_id=ident, has_side_effects=True),
    )(top, piece, x)
    return g, xo.reshape(x.shape[0], SIDE * SIDE * x.shape[1], x.shape[2])


def invert_tiles(tiles):
    k = lax.broadcasted_iota(jnp.int32, tiles[0].shape, 0)
    r = lax.broadcasted_iota(jnp.int32, tiles[0].shape, 1)
    eye = jnp.where(k == r, 1.0, 0.0).astype(jnp.float32)
    strict = [jnp.where(k < r, tile, 0.0) for tile in tiles]
    power = [jnp.where(k // 16 == r // 16, -tile, 0.0) for tile in strict]
    inverse = [eye + tile for tile in power]
    for _ in range(3):
        power = [mul(tile, tile) for tile in power]
        inverse = [one + mul(one, tile) for one, tile in zip(inverse, power)]
    for size in (16, 32, 64):
        pick = (k // (2 * size) == r // (2 * size)) & (k // size != r // size)
        half = [mul(jnp.where(pick, tile, 0.0), one) for tile, one in zip(strict, inverse)]
        inverse = [one - mul(one, tile) for one, tile in zip(inverse, half)]
    return inverse


def finish_kernel(ticks, f_ref, full_ref, t_ref, base_ref, touched_ref, ints_ref, place_ref, moved_ref,
                  out_ref, inv_ref, u_ref):
    width = f_ref.shape[1]
    tiles = width // TILE
    inv_ref[...] = jnp.zeros_like(inv_ref)

    def invert(b, carry):
        spots = [pl.ds(j * TILE, TILE) for j in range(tiles)]
        for spot, one in zip(spots, invert_tiles([f_ref[b, spot, spot] for spot in spots])):
            inv_ref[b, spot, spot] = one
        return carry

    lax.fori_loop(0, ticks, invert, 0)
    size = TILE
    while size < width:
        spots = [
            (b, pl.ds(low, size), pl.ds(low + size, size))
            for b in range(ticks) for low in range(0, width, 2 * size)
        ]
        half = [mul(f_ref[b, near, far], inv_ref[b, far, far]) for b, near, far in spots]
        for (b, near, far), tile in zip(spots, half):
            inv_ref[b, near, far] = -mul(inv_ref[b, near, near], tile)
        size *= 2

    off = ticks
    for b in range(ticks):
        rhs = t_ref[pl.ds(b * width, width), :].T
        for j in range(b):
            rhs = rhs - mul(u_ref[j], f_ref[off])
            off += 1
        u_ref[b] = mul(rhs, inv_ref[b])

    me = ints_ref[PATCH]

    @pl.when(me < ticks)
    def _():
        out_ref[...] = u_ref[jnp.minimum(me, ticks - 1)].T

    @pl.when(me >= ticks)
    def _():
        out_ref[...] = base_ref[...]

        def place_row(s, carry):
            to = ints_ref[s]

            @pl.when(to >= 0)
            def _():
                out_ref[pl.ds(to, 1), :] = touched_ref[pl.ds(s, 1), :]

            return carry

        lax.fori_loop(0, PATCH, place_row, 0)
        s = lax.broadcasted_iota(jnp.int32, (PATCH, place_ref.shape[1]), 0)
        pick = jnp.where(place_ref[0:1, :] == s, 1.0, 0.0).astype(jnp.bfloat16)
        total = None
        for k in range(ticks):
            left = full_ref[k]
            if k < ticks - 1:
                high, low = split(f_ref[off, :, pl.ds(k * PATCH, PATCH)])
                new = jnp.dot(high, pick, preferred_element_type=jnp.float32)
                new = new + jnp.dot(low, pick, preferred_element_type=jnp.float32)
                left = jnp.where(moved_ref[k:k + 1, :] > 0, new, left)
            part = mul(u_ref[k], left)
            total = part if total is None else total + part
        out_ref[...] = out_ref[...] - total.T


def finish(ticks, factor, full, t, base, touched, ints, place, moved):
    vmem = pl.BlockSpec(memory_space=pltpu.VMEM)
    width, cols = factor.shape[1], t.shape[1]
    return pl.pallas_call(
        functools.partial(finish_kernel, ticks),
        out_shape=jax.ShapeDtypeStruct(base.shape, jnp.float32),
        in_specs=[vmem] * 5 + [pl.BlockSpec(memory_space=pltpu.SMEM), vmem, vmem],
        out_specs=vmem,
        scratch_shapes=[
            pltpu.VMEM((ticks, width, width), jnp.float32), pltpu.VMEM((ticks, cols, width), jnp.float32)
        ],
        compiler_params=pltpu.CompilerParams(vmem_limit_bytes=50 * 1024 * 1024),
    )(factor, full, t, base, touched, ints, place, moved)


def find(a, b, base):
    i = jnp.arange(b.shape[0], dtype=jnp.int32)
    return jnp.max(jnp.where(a[:, None] == b[None, :], base + i[None, :], -1), axis=1)


def packing(pivots, rows):
    src = pivots.reshape(-1)
    owner = src // rows
    e = jnp.arange(src.shape[0], dtype=jnp.int32)
    same = (owner[:, None] == owner[None, :]) & (e[None, :] < e[:, None])
    return src, owner, jnp.sum(same.astype(jnp.int32), axis=1)


def rows_of(array, index):
    return jnp.take(array, index, axis=0, mode="clip")


def update(packed, owners, slab, panels, pivots, packs):
    rows, cols = slab.shape
    ticks, width = pivots.shape
    depth = panels.shape[2]
    me = lax.axis_index("row")
    src, owner, rank = packs
    top = ticks * width
    ident = 0 if packed else 2
    panel_rows = jnp.concatenate(
        [panels[k] for k in range(ticks)] + [jnp.zeros((rows, 128 - ticks * depth), jnp.float32)], axis=1
    )
    if packed:
        count, tops, space = SLOTS, ticks, pltpu.VMEM
        g = jnp.where(owner < ticks, src, top + owner * count + rank)
        s = jnp.arange(count, dtype=jnp.int32)
        held = (owner[None, :] == me) & (rank[None, :] == s[:, None])
        listed = jnp.max(jnp.where(held, src[None, :] - me * rows, 0), axis=1)
        panel_piece, slab_piece = rows_of(panel_rows, listed), rows_of(slab, listed)
    else:
        count, tops, space = rows, 0, pl.ANY
        g = src
        panel_piece, slab_piece = panel_rows, slab
    x_panels = jnp.transpose(panels, (0, 2, 1))
    g_panel, full = exchange(panel_rows, panel_piece, x_panels, tops, owners, ident, LAG, CHUNKS, space)

    s0, s1, s2 = pivots
    g0, g1, g2 = g[:width], g[width:2 * width], g[2 * width:]
    back = find(s2, s1, width)
    f2 = find(jnp.where(back >= 0, back, s2), s0, 0)
    f1 = find(s1, s0, 0)
    row20 = jnp.where(back >= 0, back, g2)
    take_t = jnp.concatenate([g0, jnp.where(f1 >= 0, f1, g1), jnp.where(f2 >= 0, f2, row20)])
    mine = me * rows + jnp.arange(rows, dtype=jnp.int32)
    h2 = find(mine, s2, 2 * width)
    pos1 = jnp.where(h2 >= 0, h2, mine)
    h1 = find(pos1, s1, width)
    pos0 = jnp.where(h1 >= 0, h1, pos1)
    h0 = find(pos0, s0, 0)
    orig = jnp.where(h0 >= 0, h0, pos0)
    moved0, moved1 = pos0 != mine, pos1 != mine
    touched = orig != mine
    q = jnp.arange(rows, dtype=jnp.int32)
    if packed:
        place = jnp.sum(((q[None, :] < q[:, None]) & touched[None, :]).astype(jnp.int32), axis=1)
        place = jnp.where(touched, place, -1)
        s = jnp.arange(PATCH, dtype=jnp.int32)
        pick = place[None, :] == s[:, None]
        to = jnp.max(jnp.where(pick, q[None, :], -1), axis=1)
        from0 = jnp.max(jnp.where(pick & moved0[None, :], pos0[None, :], 0), axis=1)
        from1 = jnp.max(jnp.where(pick & moved1[None, :], pos1[None, :], 0), axis=1)
        from_slab = jnp.max(jnp.where(pick, orig[None, :], 0), axis=1)
    else:
        from0, from1 = pos0, pos1

    def block(index, k):
        return rows_of(g_panel, index)[:, k * depth:(k + 1) * depth].T

    corner = [g_panel[k * width:(k + 1) * width, k * depth:(k + 1) * depth].T for k in range(ticks)]
    corner += [block(g1, 0), block(row20, 0), block(g2, 1)]
    if packed:
        wide = jnp.zeros((depth, width - 2 * PATCH), jnp.float32)
        corner += [jnp.concatenate([block(from0, 0), block(from1, 1), wide], axis=1)]
    else:
        corner += [block(from0, 0), block(from1, 1)]
    g_slab, factor = exchange(slab, slab_piece, jnp.stack(corner), tops, owners, ident + 1, LAG, CHUNKS, space)
    t = rows_of(g_slab, take_t)
    if packed:
        base, replaced = slab, rows_of(g_slab, from_slab)
        moved = jnp.stack([moved0, moved1] + [touched] * 6).astype(jnp.int32)
    else:
        base = jnp.where(touched[:, None], rows_of(g_slab, orig), slab)
        full = jnp.stack([
            jnp.where(moved0[None, :], factor[2 * ticks], full[0]),
            jnp.where(moved1[None, :], factor[2 * ticks + 1], full[1]),
            full[2],
        ])
        factor = factor[:2 * ticks + 1]
        moved = jnp.zeros((8, rows), jnp.int32)
        place, to = jnp.full((rows,), -1, jnp.int32), jnp.full((PATCH,), -1, jnp.int32)
        replaced = jnp.zeros((PATCH, cols), jnp.float32)
    ints = jnp.concatenate([to, jnp.full((8,), me, jnp.int32)])
    place = jnp.broadcast_to(place[None, :], (8, rows))
    return factor, full, t, base, replaced, ints, place, moved


def solution(mesh):
    owners = mesh.shape["row"]

    def local(slab, panels, pivots):
        rows, ticks = slab.shape[0], pivots.shape[0]
        packs = packing(pivots, rows)
        _, owner, rank = packs
        fits = jnp.all((owner < ticks) | (rank < SLOTS))
        ready = update(True, owners, slab, panels, pivots, packs)
        return lax.cond(
            fits,
            lambda ready, rest: finish(ticks, *ready),
            lambda ready, rest: finish(ticks, *update(False, owners, *rest)),
            ready, (slab, panels, pivots, packs),
        )

    in_specs = (P("row", "col"), P(None, "row", "col"), P())
    return jax.shard_map(local, mesh=mesh, in_specs=in_specs, out_specs=P("row", "col"), check_vma=False)
```

```python
import functools

import jax
import jax.numpy as jnp
from jax import lax
from jax.experimental import pallas as pl
from jax.experimental.pallas import tpu as pltpu
from jax.sharding import PartitionSpec as P

MESH = pl.DeviceIdType.MESH
SIDE = 4
SLOTS = 64
CHUNKS = 8
LAG = 4
SPREAD = 16
TILE = 128
PATCH = 128


def split(a):
    high = a.astype(jnp.bfloat16)
    return high, (a - high.astype(jnp.float32)).astype(jnp.bfloat16)


def mul(a, b):
    dot = functools.partial(jnp.dot, preferred_element_type=jnp.float32)
    (ah, al), (bh, bl) = split(a), split(b)
    return dot(ah, bh) + (dot(ah, bl) + dot(al, bh))


def remote(src, dst, send, recv, device):
    return pltpu.make_async_remote_copy(
        src_ref=src, dst_ref=dst, send_sem=send, recv_sem=recv, device_id=device, device_id_type=MESH
    )


class Place:
    def __init__(self, z_size):
        self.row, self.col = lax.axis_index("row"), lax.axis_index("col")
        self.z, self.core, self.z_size = self.row // 2, self.row % 2, z_size
        self.xx, self.yy = self.col // SIDE, self.col % SIDE
        self.up = (2 * ((self.z + 1) % z_size) + self.core, self.col)
        self.down = (2 * ((self.z + z_size - 1) % z_size) + self.core, self.col)
        self.partner = (2 * self.z + 1 - self.core, self.col)

    def side(self, step_x, step_y):
        return (self.row, ((self.xx + step_x) % SIDE) * SIDE + (self.yy + step_y) % SIDE)

    def greet(self):
        barrier = pltpu.get_barrier_semaphore()
        near = (self.up, self.down, self.partner)
        near += (self.side(1, 0), self.side(SIDE - 1, 0), self.side(0, 1), self.side(0, SIDE - 1))
        for device in near:
            pl.semaphore_signal(barrier, inc=1, device_id=device, device_id_type=MESH)
        pl.semaphore_wait(barrier, len(near))


class Ring:
    def __init__(self, place, tops, top_ref, piece_ref, g_ref, sems):
        self.p, self.tops, self.top_ref, self.piece_ref, self.g = place, tops, top_ref, piece_ref, g_ref
        (self.up_s, self.up_r, self.down_s, self.down_r, self.pr_s, self.pr_r,
         self.top_r, self.tu_s, self.td_s, self.tc_s, self.loc) = sems
        self.count, self.height = piece_ref.shape[0], top_ref.shape[0]
        self.chunk = self.height // CHUNKS
        self.ups = place.z_size // 2
        self.downs = place.z_size - 1 - self.ups
        self.total = LAG * self.ups + (CHUNKS if tops else 1)

    def slot(self, z, core):
        at = self.tops * self.height + (2 * (z % self.p.z_size) + core) * self.count
        return self.g.at[pl.ds(pl.multiple_of(at, 8), self.count), :]

    def hop(self, s, way, got=False):
        back = s + 1 if got else s
        if way == "up":
            ref = self.slot(self.p.z + self.p.z_size - back, self.p.core)
            return remote(ref, ref, self.up_s.at[s], self.up_r.at[s], self.p.up)
        ref = self.slot(self.p.z + back, self.p.core)
        return remote(ref, ref, self.down_s.at[s], self.down_r.at[s], self.p.down)

    def share(self, hops, got=False):
        core = 1 - self.p.core if got else self.p.core
        ref = self.slot(self.p.z + self.p.z_size - hops, core)
        return remote(ref, ref, self.pr_s.at[hops], self.pr_r.at[hops], self.p.partner)

    def top_roles(self, b):
        h = (self.p.z + self.p.z_size - b // 2) % self.p.z_size
        hops = jnp.where(h <= self.ups, h, self.p.z_size - h)
        mine = self.p.core == b % 2
        return mine, mine & (h < self.ups), mine & ((h == 0) | (h > self.ups + 1)), mine & (h > 0), hops

    def top_copy(self, b, i, kind):
        ref = self.g.at[pl.ds(pl.multiple_of(b * self.height + i * self.chunk, 8), self.chunk), :]
        send, device = {
            "up": (self.tu_s, self.p.up), "down": (self.td_s, self.p.down), "core": (self.tc_s, self.p.partner)
        }[kind]
        return remote(ref, ref, send.at[b, i], self.top_r.at[b, i], device)

    def place_own(self):
        own = pltpu.make_async_copy(self.piece_ref, self.slot(self.p.z, self.p.core), self.loc.at[0])
        own.start()
        for b in range(self.tops):
            @pl.when(self.p.row == b)
            def _():
                to = self.g.at[pl.ds(b * self.height, self.height), :]
                top = pltpu.make_async_copy(self.top_ref, to, self.loc.at[1])
                top.start()
                top.wait()
        own.wait()

    def begin(self):
        self.hop(0, "up").start()
        self.hop(0, "down").start()
        self.share(0).start()

    def step(self, t):
        for b in range(self.tops):
            mine, to_up, to_down, gets, hops = self.top_roles(b)
            i = t - LAG * hops
            inside = (i >= 0) & (i < CHUNKS)

            @pl.when(inside & gets)
            def _():
                self.top_copy(b, i, "up").wait_recv()

            @pl.when(inside & to_up)
            def _():
                self.top_copy(b, i, "up").start()

            @pl.when(inside & to_down)
            def _():
                self.top_copy(b, i, "down").start()

            @pl.when(inside & mine)
            def _():
                self.top_copy(b, i, "core").start()

        s = t // LAG
        now = (t % LAG == 0) & (s >= 1)

        @pl.when(now & (s <= self.ups))
        def _():
            self.hop(s - 1, "up", True).wait_recv()

            @pl.when(s < self.ups)
            def _():
                self.hop(s, "up").start()

            self.share(s).start()

        @pl.when(now & (s <= self.downs))
        def _():
            self.hop(s - 1, "down", True).wait_recv()

            @pl.when(s < self.downs)
            def _():
                self.hop(s, "down").start()

            self.share(self.p.z_size - s).start()

    def gather(self):
        def rest(s, carry):
            self.share(s, True).wait_recv()
            return carry

        lax.fori_loop(0, self.p.z_size, rest, 0)

        def chunks(i, carry):
            for b in range(self.tops):
                @pl.when(jnp.logical_not(self.top_roles(b)[0]))
                def _():
                    self.top_copy(b, i, "core").wait_recv()

            return carry

        if self.tops:
            lax.fori_loop(0, CHUNKS, chunks, 0)

    def drain(self):
        def hops(way):
            def body(s, carry):
                self.hop(s, way).wait_send()
                return carry

            return body

        def shares(s, carry):
            self.share(s).wait_send()
            return carry

        lax.fori_loop(0, self.ups, hops("up"), 0)
        lax.fori_loop(0, self.downs, hops("down"), 0)
        lax.fori_loop(0, self.p.z_size, shares, 0)

        def chunks(i, carry):
            for b in range(self.tops):
                mine, to_up, to_down, _, _ = self.top_roles(b)
                for role, kind in ((to_up, "up"), (to_down, "down"), (mine, "core")):
                    @pl.when(role)
                    def _():
                        self.top_copy(b, i, kind).wait_send()

            return carry

        if self.tops:
            lax.fori_loop(0, CHUNKS, chunks, 0)


def ring_sems(z_size, tops):
    dma, blocks = pltpu.SemaphoreType.DMA, max(tops, 1)
    return [dma((z_size,))] * 6 + [dma((blocks, CHUNKS))] * 4 + [dma((2,))]


class Torus:
    def __init__(self, place, blocks, x_ref, xo_ref, sems):
        self.p, self.blocks, self.x, self.xo = place, blocks, x_ref, xo_ref
        self.s, self.r, self.loc = sems
        self.half, self.quarter = x_ref.shape[1] // 2, x_ref.shape[1] // 4

    def place_own(self):
        return pltpu.make_async_copy(
            self.x.at[self.blocks], self.xo.at[self.blocks, self.p.xx, self.p.yy], self.loc.at[0]
        )

    def piece(self, k, first, second, part):
        x, y = (first, second) if k == 0 else (second, first)
        start, size = {"all": (0, self.half), "low": (0, self.quarter), "high": (self.quarter, self.quarter)}[part]
        return self.xo.at[
            self.blocks, (self.p.xx + x) % SIDE, (self.p.yy + y) % SIDE, pl.ds(k * self.half + start, size), :
        ]

    def copy(self, k, stage, v, e, receive=False):
        first = (0, SIDE - 1, 1, 2)[v]
        there, part = {0: (0, "all"), 1: (0, "all"), 2: (SIDE - 1, "low"), 3: (1, "high")}[e]
        here = (SIDE - 1, 1, 2, 2)[e]
        step = 1 if e in (0, 2) else SIDE - 1
        device = self.p.side(step, 0) if (k == 0) == (stage == 0) else self.p.side(0, step)
        n = (k * 5 + (0 if stage == 0 else 1 + v)) * 4 + e
        at = here if receive else there
        ref = self.piece(k, at, 0, part) if stage == 0 else self.piece(k, first, at, part)
        src = ref
        if e < 2 and (stage == 0 or v == 0) and not receive:
            src = self.x.at[self.blocks, pl.ds(k * self.half, self.half), :]
        return remote(src, ref, self.s.at[n], self.r.at[n], device)

    def start(self, stage, v, es):
        for e in es:
            for k in range(2):
                self.copy(k, stage, v, e).start()

    def arrive(self, stage, v, e):
        for k in range(2):
            self.copy(k, stage, v, e, True).wait_recv()

    def begin(self):
        self.start(0, 0, (0, 1))
        self.start(1, 0, (0, 1))

    def pass_on(self, stage, v):
        self.arrive(stage, v, 0)
        self.start(stage, v, (2,))
        self.arrive(stage, v, 1)
        self.start(stage, v, (3,))

    def event(self, number):
        if number == 0:
            self.arrive(0, 0, 0)
            self.start(0, 0, (2,))
            self.start(1, 1, (0, 1))
            self.arrive(0, 0, 1)
            self.start(0, 0, (3,))
            self.start(1, 2, (0, 1))
        elif number == 1:
            self.pass_on(1, 0)
        elif number == 2:
            self.arrive(0, 0, 2)
            self.arrive(0, 0, 3)
            self.start(1, 3, (0, 1))
        elif number < 6:
            self.pass_on(1, number - 2)

    def complete(self, v):
        self.arrive(1, v, 2)
        self.arrive(1, v, 3)

    def drain(self):
        for k in range(2):
            for e in range(4):
                self.copy(k, 0, 0, e).wait_send()
                for v in range(4):
                    self.copy(k, 1, v, e).wait_send()


def torus_sems():
    return [pltpu.SemaphoreType.DMA((40,))] * 2 + [pltpu.SemaphoreType.DMA((1,))]


def run(begin, end, *steps):
    def body(t, carry):
        for step in steps:
            step(t)
        return carry

    lax.fori_loop(begin, end, body, 0)


def plain_kernel(z_size, piece_ref, x_ref, g_ref, xo_ref, *sems):
    place = Place(z_size)
    place.greet()
    ring = Ring(place, 0, piece_ref, piece_ref, g_ref, sems[:11])
    torus = Torus(place, pl.ds(0, x_ref.shape[0]), x_ref, xo_ref, sems[11:])
    own = torus.place_own()
    own.start()
    torus.begin()
    ring.place_own()
    ring.begin()
    own.wait()
    run(0, ring.total, ring.step)
    for number in range(6):
        torus.event(number)
    for v in range(4):
        torus.complete(v)
    ring.gather()
    ring.drain()
    torus.drain()


def exchange(piece, x, owners, ident):
    vmem, hbm = pl.BlockSpec(memory_space=pltpu.VMEM), pl.BlockSpec(memory_space=pl.ANY)
    g, xo = pl.pallas_call(
        functools.partial(plain_kernel, owners // 2),
        out_shape=(
            jax.ShapeDtypeStruct((owners * piece.shape[0], piece.shape[1]), jnp.float32),
            jax.ShapeDtypeStruct((x.shape[0], SIDE, SIDE) + x.shape[1:], jnp.float32),
        ),
        in_specs=[vmem, vmem],
        out_specs=(hbm, hbm),
        scratch_shapes=ring_sems(owners // 2, 0) + torus_sems(),
        compiler_params=pltpu.CompilerParams(collective_id=ident, has_side_effects=True),
    )(piece, x)
    return g, xo.reshape(x.shape[0], SIDE * SIDE * x.shape[1], x.shape[2])


def packed_kernel(ticks, z_size, index_ref, ptop_ref, ppiece_ref, stop_ref, spiece_ref, x_ref,
                  gs_ref, full_ref, f_ref, gp_ref, rows_ref, y_ref, sh_s, sh_r, *sems):
    place = Place(z_size)
    place.greet()
    panel = Ring(place, ticks, ptop_ref, ppiece_ref, gp_ref, sems[:11])
    slab = Ring(place, ticks, stop_ref, spiece_ref, gs_ref, sems[11:22])
    torus = Torus(place, pl.ds(0, ticks), x_ref, full_ref, sems[22:25])
    mine = (ticks + 1) * place.core
    corner = Torus(place, pl.ds(mine, ticks + 1), y_ref, f_ref, sems[25:])
    depth, width = y_ref.shape[1:]

    own = torus.place_own()
    own.start()
    torus.begin()
    panel.place_own()
    panel.begin()
    slab.place_own()
    own.wait()
    total = panel.total
    shift = total - SPREAD
    begin = 0
    for number in range(7):
        end = total if number == 6 else 2 + (total - 2) * number // 6
        for low, high, both in ((begin, min(end, shift), False), (max(begin, shift), end, True)):
            if low < high:
                if both and low == shift:
                    slab.begin()
                steps = (panel.step,) + ((lambda t: slab.step(t - shift),) if both else ())
                run(low, high, *steps)
        begin = end
        torus.event(number)
    panel.gather()

    def load(i, carry):
        for n in range(8):
            at = i * 8 + n
            rows_ref[pl.ds(at, 1), :] = gp_ref[pl.ds(index_ref[at], 1), :]
        return carry

    lax.fori_loop(0, rows_ref.shape[0] // 8, load, 0)
    for k in range(ticks):
        y_ref[k] = gp_ref[pl.ds(k * width, width), :].T[k * depth:(k + 1) * depth]
    for n, k in ((0, 0), (1, 0), (2, 1)):
        y_ref[ticks + 1 + n] = rows_ref[pl.ds(n * width, width), :].T[k * depth:(k + 1) * depth]
    patches = rows_ref[pl.ds(3 * width, 2 * PATCH), :].T
    zeros = jnp.zeros((depth, width - 2 * PATCH), jnp.float32)
    y_ref[mine + ticks] = jnp.concatenate([patches[:depth, :PATCH], patches[depth:2 * depth, PATCH:], zeros], axis=1)

    run(total, total + 2, lambda t: slab.step(t - shift))
    own = corner.place_own()
    own.start()
    corner.begin()
    own.wait()
    begin, last = total + 2, total + shift

    def pass_share(k, v, receive=False):
        first = (0, SIDE - 1, 1, 2)[v]
        to = pl.ds((ticks + 1) * (1 - place.core if receive else place.core), ticks)
        half = pl.ds(k * corner.half, corner.half)
        if k == 0:
            ref = f_ref.at[to, (place.xx + first) % SIDE, :, half, :]
        else:
            ref = f_ref.at[to, :, (place.yy + first) % SIDE, half, :]
        return remote(ref, ref, sh_s.at[k, v], sh_r.at[k, v], place.partner)

    for number in range(7):
        end = last if number == 6 else begin + (last - begin) // (7 - number)
        if begin < end:
            run(begin, end, lambda t: slab.step(t - shift))
        begin = end
        corner.event(number)
        if number >= 4:
            v = number - 4
            corner.complete(v)
            for k in range(2):
                pass_share(k, v).start()
    corner.complete(3)
    for k in range(2):
        pass_share(k, 3).start()
    slab.gather()
    for v in range(4):
        torus.complete(v)
    for v in range(4):
        for k in range(2):
            pass_share(k, v, True).wait_recv()
            pass_share(k, v).wait_send()
    panel.drain()
    slab.drain()
    torus.drain()
    corner.drain()


def packed_exchange(index, ptop, ppiece, stop, spiece, x, ticks, owners, ident):
    vmem = pl.BlockSpec(memory_space=pltpu.VMEM)
    z_size, blocks = owners // 2, 2 * (ticks + 1)
    packed = ticks * ptop.shape[0] + owners * ppiece.shape[0]
    torus = (SIDE, SIDE) + x.shape[1:]
    f32 = jnp.float32
    gs, full, f = pl.pallas_call(
        functools.partial(packed_kernel, ticks, z_size),
        out_shape=(
            jax.ShapeDtypeStruct((packed, stop.shape[1]), f32),
            jax.ShapeDtypeStruct((ticks,) + torus, f32),
            jax.ShapeDtypeStruct((blocks,) + torus, f32),
        ),
        in_specs=[pl.BlockSpec(memory_space=pltpu.SMEM)] + [vmem] * 5,
        out_specs=(vmem, vmem, vmem),
        scratch_shapes=[
            pltpu.VMEM((packed, ptop.shape[1]), f32),
            pltpu.VMEM((index.shape[0], ptop.shape[1]), f32),
            pltpu.VMEM((blocks,) + x.shape[1:], f32),
            pltpu.SemaphoreType.DMA((2, 4)), pltpu.SemaphoreType.DMA((2, 4)),
        ] + ring_sems(z_size, ticks) * 2 + torus_sems() * 2,
        compiler_params=pltpu.CompilerParams(collective_id=ident, has_side_effects=True),
    )(index, ptop, ppiece, stop, spiece, x)
    width, depth = x.shape[2], SIDE * SIDE * x.shape[1]
    return gs, full.reshape(ticks, depth, width), f.reshape(blocks, depth, width)


def invert_tiles(tiles):
    k = lax.broadcasted_iota(jnp.int32, tiles[0].shape, 0)
    r = lax.broadcasted_iota(jnp.int32, tiles[0].shape, 1)
    eye = jnp.where(k == r, 1.0, 0.0).astype(jnp.float32)
    strict = [jnp.where(k < r, tile, 0.0) for tile in tiles]
    power = [jnp.where(k // 16 == r // 16, -tile, 0.0) for tile in strict]
    inverse = [eye + tile for tile in power]
    for _ in range(3):
        power = [mul(tile, tile) for tile in power]
        inverse = [one + mul(one, tile) for one, tile in zip(inverse, power)]
    for size in (16, 32, 64):
        pick = (k // (2 * size) == r // (2 * size)) & (k // size != r // size)
        half = [mul(jnp.where(pick, tile, 0.0), one) for tile, one in zip(strict, inverse)]
        inverse = [one - mul(one, tile) for one, tile in zip(inverse, half)]
    return inverse


def finish_kernel(ticks, f_ref, full_ref, t_ref, base_ref, touched_ref, ints_ref, place_ref, moved_ref,
                  out_ref, inv_ref, u_ref):
    width = f_ref.shape[1]
    tiles = width // TILE
    inv_ref[...] = jnp.zeros_like(inv_ref)

    def invert(b, carry):
        spots = [pl.ds(j * TILE, TILE) for j in range(tiles)]
        for spot, one in zip(spots, invert_tiles([f_ref[b, spot, spot] for spot in spots])):
            inv_ref[b, spot, spot] = one
        return carry

    lax.fori_loop(0, ticks, invert, 0)
    size = TILE
    while size < width:
        spots = [
            (b, pl.ds(low, size), pl.ds(low + size, size))
            for b in range(ticks) for low in range(0, width, 2 * size)
        ]
        half = [mul(f_ref[b, near, far], inv_ref[b, far, far]) for b, near, far in spots]
        for (b, near, far), tile in zip(spots, half):
            inv_ref[b, near, far] = -mul(inv_ref[b, near, near], tile)
        size *= 2

    off = ticks + 1
    for b in range(ticks):
        rhs = t_ref[pl.ds(b * width, width), :].T
        for j in range(b):
            rhs = rhs - mul(u_ref[j], f_ref[off])
            off += 1
        u_ref[b] = mul(rhs, inv_ref[b])

    me = ints_ref[PATCH]

    @pl.when(me < ticks)
    def _():
        out_ref[...] = u_ref[jnp.minimum(me, ticks - 1)].T

    @pl.when(me >= ticks)
    def _():
        out_ref[...] = base_ref[...]

        def place_row(s, carry):
            to = ints_ref[s]

            @pl.when(to >= 0)
            def _():
                out_ref[pl.ds(to, 1), :] = touched_ref[pl.ds(s, 1), :]

            return carry

        lax.fori_loop(0, PATCH, place_row, 0)
        s = lax.broadcasted_iota(jnp.int32, (PATCH, place_ref.shape[1]), 0)
        pick = jnp.where(place_ref[0:1, :] == s, 1.0, 0.0).astype(jnp.bfloat16)
        total = None
        for k in range(ticks):
            left = full_ref[k]
            if k < ticks - 1:
                high, low = split(f_ref[ticks + (ticks + 1) * (me % 2), :, pl.ds(k * PATCH, PATCH)])
                new = jnp.dot(high, pick, preferred_element_type=jnp.float32)
                new = new + jnp.dot(low, pick, preferred_element_type=jnp.float32)
                left = jnp.where(moved_ref[k:k + 1, :] > 0, new, left)
            part = mul(u_ref[k], left)
            total = part if total is None else total + part
        out_ref[...] = out_ref[...] - total.T


def finish(ticks, factor, full, t, base, touched, ints, place, moved):
    vmem = pl.BlockSpec(memory_space=pltpu.VMEM)
    width, cols = factor.shape[1], t.shape[1]
    return pl.pallas_call(
        functools.partial(finish_kernel, ticks),
        out_shape=jax.ShapeDtypeStruct(base.shape, jnp.float32),
        in_specs=[vmem] * 5 + [pl.BlockSpec(memory_space=pltpu.SMEM), vmem, vmem],
        out_specs=vmem,
        scratch_shapes=[
            pltpu.VMEM((ticks, width, width), jnp.float32), pltpu.VMEM((ticks, cols, width), jnp.float32)
        ],
        compiler_params=pltpu.CompilerParams(vmem_limit_bytes=50 * 1024 * 1024),
    )(factor, full, t, base, touched, ints, place, moved)


def find(a, b, base):
    i = jnp.arange(b.shape[0], dtype=jnp.int32)
    return jnp.max(jnp.where(a[:, None] == b[None, :], base + i[None, :], -1), axis=1)


def packing(pivots, rows):
    src = pivots.reshape(-1)
    owner = src // rows
    e = jnp.arange(src.shape[0], dtype=jnp.int32)
    same = (owner[:, None] == owner[None, :]) & (e[None, :] < e[:, None])
    return src, owner, jnp.sum(same.astype(jnp.int32), axis=1)


def rows_of(array, index):
    return jnp.take(array, index, axis=0, mode="clip")


def update(packed, owners, slab, panels, pivots, packs):
    rows, cols = slab.shape
    ticks, width = pivots.shape
    depth = panels.shape[2]
    me = lax.axis_index("row")
    src, owner, rank = packs
    top = ticks * width
    panel_rows = jnp.concatenate(
        [panels[k] for k in range(ticks)] + [jnp.zeros((rows, 128 - ticks * depth), jnp.float32)], axis=1
    )
    g = src
    if packed:
        g = jnp.where(owner < ticks, src, top + jnp.minimum(owner * SLOTS + rank, owners * SLOTS - 1))
        s = jnp.arange(SLOTS, dtype=jnp.int32)
        held = (owner[None, :] == me) & (rank[None, :] == s[:, None])
        listed = jnp.max(jnp.where(held, src[None, :] - me * rows, 0), axis=1)
    x_panels = jnp.transpose(panels, (0, 2, 1))

    s0, s1, s2 = pivots
    g0, g1, g2 = g[:width], g[width:2 * width], g[2 * width:]
    back = find(s2, s1, width)
    f2 = find(jnp.where(back >= 0, back, s2), s0, 0)
    f1 = find(s1, s0, 0)
    row20 = jnp.where(back >= 0, back, g2)
    take_t = jnp.concatenate([g0, jnp.where(f1 >= 0, f1, g1), jnp.where(f2 >= 0, f2, row20)])
    mine = me * rows + jnp.arange(rows, dtype=jnp.int32)
    h2 = find(mine, s2, 2 * width)
    pos1 = jnp.where(h2 >= 0, h2, mine)
    h1 = find(pos1, s1, width)
    pos0 = jnp.where(h1 >= 0, h1, pos1)
    h0 = find(pos0, s0, 0)
    orig = jnp.where(h0 >= 0, h0, pos0)
    moved0, moved1 = pos0 != mine, pos1 != mine
    touched = orig != mine
    q = jnp.arange(rows, dtype=jnp.int32)
    if packed:
        place = jnp.sum(((q[None, :] < q[:, None]) & touched[None, :]).astype(jnp.int32), axis=1)
        place = jnp.where(touched, place, -1)
        s = jnp.arange(PATCH, dtype=jnp.int32)
        pick = place[None, :] == s[:, None]
        to = jnp.max(jnp.where(pick, q[None, :], -1), axis=1)
        from0 = jnp.max(jnp.where(pick & moved0[None, :], pos0[None, :], 0), axis=1)
        from1 = jnp.max(jnp.where(pick & moved1[None, :], pos1[None, :], 0), axis=1)
        from_slab = jnp.max(jnp.where(pick, orig[None, :], 0), axis=1)
    else:
        from0, from1 = pos0, pos1

    if packed:
        index = jnp.concatenate([g1, row20, g2, from0, from1])
        g_slab, full, factor = packed_exchange(
            index, panel_rows, rows_of(panel_rows, listed), slab, rows_of(slab, listed), x_panels, ticks, owners, 0
        )
        base, replaced = slab, rows_of(g_slab, from_slab)
        moved = jnp.stack([moved0, moved1] + [touched] * 6).astype(jnp.int32)
    else:
        g_panel, full = exchange(panel_rows, x_panels, owners, 1)

        def block(index, k):
            return rows_of(g_panel, index)[:, k * depth:(k + 1) * depth].T

        corner = [g_panel[k * width:(k + 1) * width, k * depth:(k + 1) * depth].T for k in range(ticks)]
        corner += [block(from0, 0), block(g1, 0), block(row20, 0), block(g2, 1), block(from1, 1)]
        g_slab, factor = exchange(slab, jnp.stack(corner), owners, 2)
        base = jnp.where(touched[:, None], rows_of(g_slab, orig), slab)
        full = jnp.stack([
            jnp.where(moved0[None, :], factor[ticks], full[0]),
            jnp.where(moved1[None, :], factor[2 * ticks + 1], full[1]),
            full[2],
        ])
        moved = jnp.zeros((8, rows), jnp.int32)
        place, to = jnp.full((rows,), -1, jnp.int32), jnp.full((PATCH,), -1, jnp.int32)
        replaced = jnp.zeros((PATCH, cols), jnp.float32)
    t = rows_of(g_slab, take_t)
    ints = jnp.concatenate([to, jnp.full((8,), me, jnp.int32)])
    place = jnp.broadcast_to(place[None, :], (8, rows))
    return factor, full, t, base, replaced, ints, place, moved


def solution(mesh):
    owners = mesh.shape["row"]

    def local(slab, panels, pivots):
        rows, ticks = slab.shape[0], pivots.shape[0]
        packs = packing(pivots, rows)
        _, owner, rank = packs
        fits = jnp.all((owner < ticks) | (rank < SLOTS))
        ready = update(True, owners, slab, panels, pivots, packs)
        return lax.cond(
            fits,
            lambda ready, rest: finish(ticks, *ready),
            lambda ready, rest: finish(ticks, *update(False, owners, *rest)),
            ready, (slab, panels, pivots, packs),
        )

    in_specs = (P("row", "col"), P(None, "row", "col"), P())
    return jax.shard_map(local, mesh=mesh, in_specs=in_specs, out_specs=P("row", "col"), check_vma=False)
```

```python
import functools

import jax
import jax.numpy as jnp
from jax import lax
from jax.experimental import pallas as pl
from jax.experimental.pallas import tpu as pltpu
from jax.sharding import PartitionSpec as P

MESH = pl.DeviceIdType.MESH
SIDE = 4
SLOTS = 64
CHUNKS = 8
LAG = 4
SPREAD = 16
TILE = 128
PATCH = 128


def split(a):
    high = a.astype(jnp.bfloat16)
    return high, (a - high.astype(jnp.float32)).astype(jnp.bfloat16)


def mul(a, b):
    dot = functools.partial(jnp.dot, preferred_element_type=jnp.float32)
    (ah, al), (bh, bl) = split(a), split(b)
    return dot(ah, bh) + (dot(ah, bl) + dot(al, bh))


def remote(src, dst, send, recv, device):
    return pltpu.make_async_remote_copy(
        src_ref=src, dst_ref=dst, send_sem=send, recv_sem=recv, device_id=device, device_id_type=MESH
    )


class Place:
    def __init__(self, z_size):
        self.row, self.col = lax.axis_index("row"), lax.axis_index("col")
        self.z, self.core, self.z_size = self.row // 2, self.row % 2, z_size
        self.xx, self.yy = self.col // SIDE, self.col % SIDE
        self.up = (2 * ((self.z + 1) % z_size) + self.core, self.col)
        self.down = (2 * ((self.z + z_size - 1) % z_size) + self.core, self.col)
        self.partner = (2 * self.z + 1 - self.core, self.col)

    def side(self, step_x, step_y):
        return (self.row, ((self.xx + step_x) % SIDE) * SIDE + (self.yy + step_y) % SIDE)

    def greet(self):
        barrier = pltpu.get_barrier_semaphore()
        near = (self.up, self.down, self.partner)
        near += (self.side(1, 0), self.side(SIDE - 1, 0), self.side(0, 1), self.side(0, SIDE - 1))
        for device in near:
            pl.semaphore_signal(barrier, inc=1, device_id=device, device_id_type=MESH)
        pl.semaphore_wait(barrier, len(near))


class Ring:
    def __init__(self, place, tops, top_ref, piece_ref, g_ref, sems):
        self.p, self.tops, self.top_ref, self.piece_ref, self.g = place, tops, top_ref, piece_ref, g_ref
        (self.up_s, self.up_r, self.down_s, self.down_r, self.pr_s, self.pr_r,
         self.top_r, self.tu_s, self.td_s, self.tc_s, self.loc) = sems
        self.count, self.height = piece_ref.shape[0], top_ref.shape[0]
        self.chunk = self.height // CHUNKS
        self.ups = place.z_size // 2
        self.downs = place.z_size - 1 - self.ups
        self.total = LAG * self.ups + (CHUNKS if tops else 1)

    def slot(self, z, core):
        at = self.tops * self.height + (2 * (z % self.p.z_size) + core) * self.count
        return self.g.at[pl.ds(pl.multiple_of(at, 8), self.count), :]

    def hop(self, s, way, got=False):
        back = s + 1 if got else s
        if way == "up":
            ref = self.slot(self.p.z + self.p.z_size - back, self.p.core)
            return remote(ref, ref, self.up_s.at[s], self.up_r.at[s], self.p.up)
        ref = self.slot(self.p.z + back, self.p.core)
        return remote(ref, ref, self.down_s.at[s], self.down_r.at[s], self.p.down)

    def share(self, hops, got=False):
        core = 1 - self.p.core if got else self.p.core
        ref = self.slot(self.p.z + self.p.z_size - hops, core)
        return remote(ref, ref, self.pr_s.at[hops], self.pr_r.at[hops], self.p.partner)

    def top_roles(self, b):
        h = (self.p.z + self.p.z_size - b // 2) % self.p.z_size
        hops = jnp.where(h <= self.ups, h, self.p.z_size - h)
        mine = self.p.core == b % 2
        return mine, mine & (h < self.ups), mine & ((h == 0) | (h > self.ups + 1)), mine & (h > 0), hops

    def top_copy(self, b, i, kind):
        ref = self.g.at[pl.ds(pl.multiple_of(b * self.height + i * self.chunk, 8), self.chunk), :]
        send, device = {
            "up": (self.tu_s, self.p.up), "down": (self.td_s, self.p.down), "core": (self.tc_s, self.p.partner)
        }[kind]
        return remote(ref, ref, send.at[b, i], self.top_r.at[b, i], device)

    def place_own(self):
        own = pltpu.make_async_copy(self.piece_ref, self.slot(self.p.z, self.p.core), self.loc.at[0])
        own.start()
        for b in range(self.tops):
            @pl.when(self.p.row == b)
            def _():
                to = self.g.at[pl.ds(b * self.height, self.height), :]
                top = pltpu.make_async_copy(self.top_ref, to, self.loc.at[1])
                top.start()
                top.wait()
        own.wait()

    def begin(self):
        self.hop(0, "up").start()
        self.hop(0, "down").start()
        self.share(0).start()

    def step(self, t):
        for b in range(self.tops):
            mine, to_up, to_down, gets, hops = self.top_roles(b)
            i = t - LAG * hops
            inside = (i >= 0) & (i < CHUNKS)

            @pl.when(inside & gets)
            def _():
                self.top_copy(b, i, "up").wait_recv()

            @pl.when(inside & to_up)
            def _():
                self.top_copy(b, i, "up").start()

            @pl.when(inside & to_down)
            def _():
                self.top_copy(b, i, "down").start()

            @pl.when(inside & mine)
            def _():
                self.top_copy(b, i, "core").start()

        s = t // LAG
        now = (t % LAG == 0) & (s >= 1)

        @pl.when(now & (s <= self.ups))
        def _():
            self.hop(s - 1, "up", True).wait_recv()

            @pl.when(s < self.ups)
            def _():
                self.hop(s, "up").start()

            self.share(s).start()

        @pl.when(now & (s <= self.downs))
        def _():
            self.hop(s - 1, "down", True).wait_recv()

            @pl.when(s < self.downs)
            def _():
                self.hop(s, "down").start()

            self.share(self.p.z_size - s).start()

    def gather(self):
        def rest(s, carry):
            self.share(s, True).wait_recv()
            return carry

        lax.fori_loop(0, self.p.z_size, rest, 0)

        def chunks(i, carry):
            for b in range(self.tops):
                @pl.when(jnp.logical_not(self.top_roles(b)[0]))
                def _():
                    self.top_copy(b, i, "core").wait_recv()

            return carry

        if self.tops:
            lax.fori_loop(0, CHUNKS, chunks, 0)

    def drain(self):
        def hops(way):
            def body(s, carry):
                self.hop(s, way).wait_send()
                return carry

            return body

        def shares(s, carry):
            self.share(s).wait_send()
            return carry

        lax.fori_loop(0, self.ups, hops("up"), 0)
        lax.fori_loop(0, self.downs, hops("down"), 0)
        lax.fori_loop(0, self.p.z_size, shares, 0)

        def chunks(i, carry):
            for b in range(self.tops):
                mine, to_up, to_down, _, _ = self.top_roles(b)
                for role, kind in ((to_up, "up"), (to_down, "down"), (mine, "core")):
                    @pl.when(role)
                    def _():
                        self.top_copy(b, i, kind).wait_send()

            return carry

        if self.tops:
            lax.fori_loop(0, CHUNKS, chunks, 0)


def ring_sems(z_size, tops):
    dma, blocks = pltpu.SemaphoreType.DMA, max(tops, 1)
    return [dma((z_size,))] * 6 + [dma((blocks, CHUNKS))] * 4 + [dma((2,))]


class Torus:
    def __init__(self, place, blocks, x_ref, xo_ref, sems):
        self.p, self.blocks, self.x, self.xo = place, blocks, x_ref, xo_ref
        self.s, self.r, self.loc = sems
        self.half, self.quarter = x_ref.shape[1] // 2, x_ref.shape[1] // 4

    def place_own(self):
        return pltpu.make_async_copy(
            self.x.at[self.blocks], self.xo.at[self.blocks, self.p.xx, self.p.yy], self.loc.at[0]
        )

    def piece(self, k, first, second, part):
        x, y = (first, second) if k == 0 else (second, first)
        start, size = {"all": (0, self.half), "low": (0, self.quarter), "high": (self.quarter, self.quarter)}[part]
        return self.xo.at[
            self.blocks, (self.p.xx + x) % SIDE, (self.p.yy + y) % SIDE, pl.ds(k * self.half + start, size), :
        ]

    def copy(self, k, stage, v, e, receive=False):
        first = (0, SIDE - 1, 1, 2)[v]
        there, part = {0: (0, "all"), 1: (0, "all"), 2: (SIDE - 1, "low"), 3: (1, "high")}[e]
        here = (SIDE - 1, 1, 2, 2)[e]
        step = 1 if e in (0, 2) else SIDE - 1
        device = self.p.side(step, 0) if (k == 0) == (stage == 0) else self.p.side(0, step)
        n = (k * 5 + (0 if stage == 0 else 1 + v)) * 4 + e
        at = here if receive else there
        ref = self.piece(k, at, 0, part) if stage == 0 else self.piece(k, first, at, part)
        src = ref
        if e < 2 and (stage == 0 or v == 0) and not receive:
            src = self.x.at[self.blocks, pl.ds(k * self.half, self.half), :]
        return remote(src, ref, self.s.at[n], self.r.at[n], device)

    def start(self, stage, v, es):
        for e in es:
            for k in range(2):
                self.copy(k, stage, v, e).start()

    def arrive(self, stage, v, e):
        for k in range(2):
            self.copy(k, stage, v, e, True).wait_recv()

    def begin(self):
        self.start(0, 0, (0, 1))
        self.start(1, 0, (0, 1))

    def pass_on(self, stage, v):
        self.arrive(stage, v, 0)
        self.start(stage, v, (2,))
        self.arrive(stage, v, 1)
        self.start(stage, v, (3,))

    def event(self, number):
        if number == 0:
            self.arrive(0, 0, 0)
            self.start(0, 0, (2,))
            self.start(1, 1, (0, 1))
            self.arrive(0, 0, 1)
            self.start(0, 0, (3,))
            self.start(1, 2, (0, 1))
        elif number == 1:
            self.pass_on(1, 0)
        elif number == 2:
            self.arrive(0, 0, 2)
            self.arrive(0, 0, 3)
            self.start(1, 3, (0, 1))
        elif number < 6:
            self.pass_on(1, number - 2)

    def complete(self, v):
        self.arrive(1, v, 2)
        self.arrive(1, v, 3)

    def drain(self):
        for k in range(2):
            for e in range(4):
                self.copy(k, 0, 0, e).wait_send()
                for v in range(4):
                    self.copy(k, 1, v, e).wait_send()


def torus_sems():
    return [pltpu.SemaphoreType.DMA((40,))] * 2 + [pltpu.SemaphoreType.DMA((1,))]


def run(begin, end, *steps):
    def body(t, carry):
        for step in steps:
            step(t)
        return carry

    lax.fori_loop(begin, end, body, 0)


def plain_kernel(z_size, piece_ref, x_ref, g_ref, xo_ref, *sems):
    place = Place(z_size)
    place.greet()
    ring = Ring(place, 0, piece_ref, piece_ref, g_ref, sems[:11])
    torus = Torus(place, pl.ds(0, x_ref.shape[0]), x_ref, xo_ref, sems[11:])
    own = torus.place_own()
    own.start()
    torus.begin()
    ring.place_own()
    ring.begin()
    own.wait()
    run(0, ring.total, ring.step)
    for number in range(6):
        torus.event(number)
    for v in range(4):
        torus.complete(v)
    ring.gather()
    ring.drain()
    torus.drain()


def exchange(piece, x, owners, ident):
    vmem, hbm = pl.BlockSpec(memory_space=pltpu.VMEM), pl.BlockSpec(memory_space=pl.ANY)
    g, xo = pl.pallas_call(
        functools.partial(plain_kernel, owners // 2),
        out_shape=(
            jax.ShapeDtypeStruct((owners * piece.shape[0], piece.shape[1]), jnp.float32),
            jax.ShapeDtypeStruct((x.shape[0], SIDE, SIDE) + x.shape[1:], jnp.float32),
        ),
        in_specs=[vmem, vmem],
        out_specs=(hbm, hbm),
        scratch_shapes=ring_sems(owners // 2, 0) + torus_sems(),
        compiler_params=pltpu.CompilerParams(collective_id=ident, has_side_effects=True),
    )(piece, x)
    return g, xo.reshape(x.shape[0], SIDE * SIDE * x.shape[1], x.shape[2])


def packed_kernel(ticks, z_size, index_ref, take_ref, stop_ref, x_ref, full_ref, f_ref, t_ref,
                  ptop_ref, ppiece_ref, spiece_ref, gs_ref, gp_ref, rows_ref, y_ref, sh_s, sh_r, *sems):
    place = Place(z_size)
    spare = jnp.zeros((ptop_ref.shape[1] - ticks * x_ref.shape[1], x_ref.shape[2]), jnp.float32)
    ptop_ref[...] = jnp.concatenate([x_ref[k] for k in range(ticks)] + [spare], axis=0).T
    first = rows_ref.shape[0]

    def pack(i, carry):
        for n in range(8):
            at = i * 8 + n
            row = index_ref[first + at]
            ppiece_ref[pl.ds(at, 1), :] = ptop_ref[pl.ds(row, 1), :]
            spiece_ref[pl.ds(at, 1), :] = stop_ref[pl.ds(row, 1), :]
        return carry

    lax.fori_loop(0, ppiece_ref.shape[0] // 8, pack, 0)
    place.greet()
    panel = Ring(place, ticks, ptop_ref, ppiece_ref, gp_ref, sems[:11])
    slab = Ring(place, ticks, stop_ref, spiece_ref, gs_ref, sems[11:22])
    torus = Torus(place, pl.ds(0, ticks), x_ref, full_ref, sems[22:25])
    mine = (ticks + 1) * place.core
    corner = Torus(place, pl.ds(mine, ticks + 1), y_ref, f_ref, sems[25:])
    depth, width = y_ref.shape[1:]

    own = torus.place_own()
    own.start()
    torus.begin()
    panel.place_own()
    panel.begin()
    slab.place_own()
    own.wait()
    total = panel.total
    shift = total - SPREAD
    begin = 0
    for number in range(7):
        end = total if number == 6 else 2 + (total - 2) * number // 6
        for low, high, both in ((begin, min(end, shift), False), (max(begin, shift), end, True)):
            if low < high:
                if both and low == shift:
                    slab.begin()
                steps = (panel.step,) + ((lambda t: slab.step(t - shift),) if both else ())
                run(low, high, *steps)
        begin = end
        torus.event(number)
    panel.gather()

    def load(i, carry):
        for n in range(8):
            at = i * 8 + n
            rows_ref[pl.ds(at, 1), :] = gp_ref[pl.ds(index_ref[at], 1), :]
        return carry

    lax.fori_loop(0, rows_ref.shape[0] // 8, load, 0)
    for k in range(ticks):
        y_ref[k] = gp_ref[pl.ds(k * width, width), :].T[k * depth:(k + 1) * depth]
    for n, k in ((0, 0), (1, 0), (2, 1)):
        y_ref[ticks + 1 + n] = rows_ref[pl.ds(n * width, width), :].T[k * depth:(k + 1) * depth]
    patches = rows_ref[pl.ds(3 * width, 2 * PATCH), :].T
    zeros = jnp.zeros((depth, width - 2 * PATCH), jnp.float32)
    y_ref[mine + ticks] = jnp.concatenate([patches[:depth, :PATCH], patches[depth:2 * depth, PATCH:], zeros], axis=1)

    run(total, total + 2, lambda t: slab.step(t - shift))
    own = corner.place_own()
    own.start()
    corner.begin()
    own.wait()
    begin, last = total + 2, total + shift

    def pass_share(k, v, receive=False):
        first = (0, SIDE - 1, 1, 2)[v]
        to = pl.ds((ticks + 1) * (1 - place.core if receive else place.core), ticks)
        half = pl.ds(k * corner.half, corner.half)
        if k == 0:
            ref = f_ref.at[to, (place.xx + first) % SIDE, :, half, :]
        else:
            ref = f_ref.at[to, :, (place.yy + first) % SIDE, half, :]
        return remote(ref, ref, sh_s.at[k, v], sh_r.at[k, v], place.partner)

    def pick(i, carry):
        for n in range(8):
            at = i * 8 + n
            t_ref[pl.ds(at, 1), :] = gs_ref[pl.ds(take_ref[at], 1), :]
        return carry

    for number in range(7):
        end = last if number == 6 else begin + (last - begin) // (7 - number)
        if begin < end:
            run(begin, end, lambda t: slab.step(t - shift))
        begin = end
        corner.event(number)
        if number == 6:
            slab.gather()
            lax.fori_loop(0, t_ref.shape[0] // 8, pick, 0)
        if number >= 4:
            v = number - 4
            corner.complete(v)
            for k in range(2):
                pass_share(k, v).start()
    corner.complete(3)
    for k in range(2):
        pass_share(k, 3).start()
    for v in range(4):
        torus.complete(v)
    for v in range(4):
        for k in range(2):
            pass_share(k, v, True).wait_recv()
            pass_share(k, v).wait_send()
    panel.drain()
    slab.drain()
    torus.drain()
    corner.drain()


def packed_exchange(index, take, slab, x, ticks, owners, ident):
    vmem, smem = pl.BlockSpec(memory_space=pltpu.VMEM), pl.BlockSpec(memory_space=pltpu.SMEM)
    z_size, blocks = owners // 2, 2 * (ticks + 1)
    rows, cols = slab.shape
    packed = ticks * rows + owners * SLOTS
    torus = (SIDE, SIDE) + x.shape[1:]
    f32 = jnp.float32
    full, f, t = pl.pallas_call(
        functools.partial(packed_kernel, ticks, z_size),
        out_shape=(
            jax.ShapeDtypeStruct((ticks,) + torus, f32),
            jax.ShapeDtypeStruct((blocks,) + torus, f32),
            jax.ShapeDtypeStruct((take.shape[0], cols), f32),
        ),
        in_specs=[smem, smem, vmem, vmem],
        out_specs=(vmem, vmem, vmem),
        scratch_shapes=[
            pltpu.VMEM((rows, TILE), f32),
            pltpu.VMEM((SLOTS, TILE), f32),
            pltpu.VMEM((SLOTS, cols), f32),
            pltpu.VMEM((packed, cols), f32),
            pltpu.VMEM((packed, TILE), f32),
            pltpu.VMEM((index.shape[0] - SLOTS, TILE), f32),
            pltpu.VMEM((blocks,) + x.shape[1:], f32),
            pltpu.SemaphoreType.DMA((2, 4)), pltpu.SemaphoreType.DMA((2, 4)),
        ] + ring_sems(z_size, ticks) * 2 + torus_sems() * 2,
        compiler_params=pltpu.CompilerParams(collective_id=ident, has_side_effects=True),
    )(index, take, slab, x)
    width, depth = x.shape[2], SIDE * SIDE * x.shape[1]
    return full.reshape(ticks, depth, width), f.reshape(blocks, depth, width), t


def invert_tiles(tiles):
    k = lax.broadcasted_iota(jnp.int32, tiles[0].shape, 0)
    r = lax.broadcasted_iota(jnp.int32, tiles[0].shape, 1)
    eye = jnp.where(k == r, 1.0, 0.0).astype(jnp.float32)
    strict = [jnp.where(k < r, tile, 0.0) for tile in tiles]
    power = [jnp.where(k // 16 == r // 16, -tile, 0.0) for tile in strict]
    inverse = [eye + tile for tile in power]
    for _ in range(3):
        power = [mul(tile, tile) for tile in power]
        inverse = [one + mul(one, tile) for one, tile in zip(inverse, power)]
    for size in (16, 32, 64):
        pick = (k // (2 * size) == r // (2 * size)) & (k // size != r // size)
        half = [mul(jnp.where(pick, tile, 0.0), one) for tile, one in zip(strict, inverse)]
        inverse = [one - mul(one, tile) for one, tile in zip(inverse, half)]
    return inverse


def finish_kernel(ticks, f_ref, full_ref, t_ref, base_ref, ints_ref, place_ref, moved_ref,
                  out_ref, inv_ref, u_ref):
    width = f_ref.shape[1]
    tiles = width // TILE
    inv_ref[...] = jnp.zeros_like(inv_ref)

    def invert(b, carry):
        spots = [pl.ds(j * TILE, TILE) for j in range(tiles)]
        for spot, one in zip(spots, invert_tiles([f_ref[b, spot, spot] for spot in spots])):
            inv_ref[b, spot, spot] = one
        return carry

    lax.fori_loop(0, ticks, invert, 0)
    size = TILE
    while size < width:
        spots = [
            (b, pl.ds(low, size), pl.ds(low + size, size))
            for b in range(ticks) for low in range(0, width, 2 * size)
        ]
        half = [mul(f_ref[b, near, far], inv_ref[b, far, far]) for b, near, far in spots]
        for (b, near, far), tile in zip(spots, half):
            inv_ref[b, near, far] = -mul(inv_ref[b, near, near], tile)
        size *= 2

    off = ticks + 1
    for b in range(ticks):
        rhs = t_ref[pl.ds(b * width, width), :].T
        for j in range(b):
            rhs = rhs - mul(u_ref[j], f_ref[off])
            off += 1
        u_ref[b] = mul(rhs, inv_ref[b])

    me = ints_ref[PATCH]

    @pl.when(me < ticks)
    def _():
        out_ref[...] = u_ref[jnp.minimum(me, ticks - 1)].T

    @pl.when(me >= ticks)
    def _():
        out_ref[...] = base_ref[...]

        def place_row(s, carry):
            to = ints_ref[s]

            @pl.when(to >= 0)
            def _():
                out_ref[pl.ds(to, 1), :] = t_ref[pl.ds(ticks * width + s, 1), :]

            return carry

        lax.fori_loop(0, PATCH, place_row, 0)
        s = lax.broadcasted_iota(jnp.int32, (PATCH, place_ref.shape[1]), 0)
        pick = jnp.where(place_ref[0:1, :] == s, 1.0, 0.0).astype(jnp.bfloat16)
        total = None
        for k in range(ticks):
            left = full_ref[k]
            if k < ticks - 1:
                high, low = split(f_ref[ticks + (ticks + 1) * (me % 2), :, pl.ds(k * PATCH, PATCH)])
                new = jnp.dot(high, pick, preferred_element_type=jnp.float32)
                new = new + jnp.dot(low, pick, preferred_element_type=jnp.float32)
                left = jnp.where(moved_ref[k:k + 1, :] > 0, new, left)
            part = mul(u_ref[k], left)
            total = part if total is None else total + part
        out_ref[...] = out_ref[...] - total.T


def finish(ticks, factor, full, t, base, ints, place, moved):
    vmem = pl.BlockSpec(memory_space=pltpu.VMEM)
    width, cols = factor.shape[1], t.shape[1]
    return pl.pallas_call(
        functools.partial(finish_kernel, ticks),
        out_shape=jax.ShapeDtypeStruct(base.shape, jnp.float32),
        in_specs=[vmem] * 4 + [pl.BlockSpec(memory_space=pltpu.SMEM), vmem, vmem],
        out_specs=vmem,
        scratch_shapes=[
            pltpu.VMEM((ticks, width, width), jnp.float32), pltpu.VMEM((ticks, cols, width), jnp.float32)
        ],
        compiler_params=pltpu.CompilerParams(vmem_limit_bytes=50 * 1024 * 1024),
    )(factor, full, t, base, ints, place, moved)


def find(a, b, base):
    i = jnp.arange(b.shape[0], dtype=jnp.int32)
    return jnp.max(jnp.where(a[:, None] == b[None, :], base + i[None, :], -1), axis=1)


def packing(pivots, rows):
    src = pivots.reshape(-1)
    owner = src // rows
    e = jnp.arange(src.shape[0], dtype=jnp.int32)
    same = (owner[:, None] == owner[None, :]) & (e[None, :] < e[:, None])
    return src, owner, jnp.sum(same.astype(jnp.int32), axis=1)


def rows_of(array, index):
    return jnp.take(array, index, axis=0, mode="clip")


def update(packed, owners, slab, panels, pivots, packs):
    rows, cols = slab.shape
    ticks, width = pivots.shape
    depth = panels.shape[2]
    me = lax.axis_index("row")
    src, owner, rank = packs
    top = ticks * width
    g = src
    if packed:
        g = jnp.where(owner < ticks, src, top + jnp.minimum(owner * SLOTS + rank, owners * SLOTS - 1))
        s = jnp.arange(SLOTS, dtype=jnp.int32)
        held = (owner[None, :] == me) & (rank[None, :] == s[:, None])
        listed = jnp.max(jnp.where(held, src[None, :] - me * rows, 0), axis=1)
    x_panels = jnp.transpose(panels, (0, 2, 1))

    s0, s1, s2 = pivots
    g0, g1, g2 = g[:width], g[width:2 * width], g[2 * width:]
    back = find(s2, s1, width)
    f2 = find(jnp.where(back >= 0, back, s2), s0, 0)
    f1 = find(s1, s0, 0)
    row20 = jnp.where(back >= 0, back, g2)
    take_t = jnp.concatenate([g0, jnp.where(f1 >= 0, f1, g1), jnp.where(f2 >= 0, f2, row20)])
    mine = me * rows + jnp.arange(rows, dtype=jnp.int32)
    h2 = find(mine, s2, 2 * width)
    pos1 = jnp.where(h2 >= 0, h2, mine)
    h1 = find(pos1, s1, width)
    pos0 = jnp.where(h1 >= 0, h1, pos1)
    h0 = find(pos0, s0, 0)
    orig = jnp.where(h0 >= 0, h0, pos0)
    moved0, moved1 = pos0 != mine, pos1 != mine
    touched = orig != mine
    q = jnp.arange(rows, dtype=jnp.int32)
    if packed:
        place = jnp.sum(((q[None, :] < q[:, None]) & touched[None, :]).astype(jnp.int32), axis=1)
        place = jnp.where(touched, place, -1)
        s = jnp.arange(PATCH, dtype=jnp.int32)
        pick = place[None, :] == s[:, None]
        to = jnp.max(jnp.where(pick, q[None, :], -1), axis=1)
        from0 = jnp.max(jnp.where(pick & moved0[None, :], pos0[None, :], 0), axis=1)
        from1 = jnp.max(jnp.where(pick & moved1[None, :], pos1[None, :], 0), axis=1)
        from_slab = jnp.max(jnp.where(pick, orig[None, :], 0), axis=1)
    else:
        from0, from1 = pos0, pos1

    if packed:
        index = jnp.concatenate([g1, row20, g2, from0, from1, listed])
        take = jnp.concatenate([take_t, from_slab])
        full, factor, t = packed_exchange(index, take, slab, x_panels, ticks, owners, 0)
        base = slab
        moved = jnp.stack([moved0, moved1] + [touched] * 6).astype(jnp.int32)
    else:
        panel_rows = jnp.concatenate(
            [panels[k] for k in range(ticks)] + [jnp.zeros((rows, 128 - ticks * depth), jnp.float32)], axis=1
        )
        g_panel, full = exchange(panel_rows, x_panels, owners, 1)

        def block(index, k):
            return rows_of(g_panel, index)[:, k * depth:(k + 1) * depth].T

        corner = [g_panel[k * width:(k + 1) * width, k * depth:(k + 1) * depth].T for k in range(ticks)]
        corner += [block(from0, 0), block(g1, 0), block(row20, 0), block(g2, 1), block(from1, 1)]
        g_slab, factor = exchange(slab, jnp.stack(corner), owners, 2)
        base = jnp.where(touched[:, None], rows_of(g_slab, orig), slab)
        full = jnp.stack([
            jnp.where(moved0[None, :], factor[ticks], full[0]),
            jnp.where(moved1[None, :], factor[2 * ticks + 1], full[1]),
            full[2],
        ])
        moved = jnp.zeros((8, rows), jnp.int32)
        place, to = jnp.full((rows,), -1, jnp.int32), jnp.full((PATCH,), -1, jnp.int32)
        t = rows_of(g_slab, jnp.concatenate([take_t, jnp.zeros((PATCH,), jnp.int32)]))
    ints = jnp.concatenate([to, jnp.full((8,), me, jnp.int32)])
    place = jnp.broadcast_to(place[None, :], (8, rows))
    return factor, full, t, base, ints, place, moved


def solution(mesh):
    owners = mesh.shape["row"]

    def local(slab, panels, pivots):
        rows, ticks = slab.shape[0], pivots.shape[0]
        packs = packing(pivots, rows)
        _, owner, rank = packs
        fits = jnp.all((owner < ticks) | (rank < SLOTS))
        ready = update(True, owners, slab, panels, pivots, packs)
        return lax.cond(
            fits,
            lambda ready, rest: finish(ticks, *ready),
            lambda ready, rest: finish(ticks, *update(False, owners, *rest)),
            ready, (slab, panels, pivots, packs),
        )

    in_specs = (P("row", "col"), P(None, "row", "col"), P())
    return jax.shard_map(local, mesh=mesh, in_specs=in_specs, out_specs=P("row", "col"), check_vma=False)
```

```python
import functools

import jax
import jax.numpy as jnp
from jax import lax
from jax.experimental import pallas as pl
from jax.experimental.pallas import tpu as pltpu
from jax.sharding import PartitionSpec as P

MESH = pl.DeviceIdType.MESH
SIDE = 4
SLOTS = 64
CHUNKS = 8
LAG = 4
SPREAD = 16
TILE = 128
DIAGONAL, ACROSS = (0, 1, 4), (2, 5, 6)
PATCH = 128


def split(a):
    high = a.astype(jnp.bfloat16)
    return high, (a - high.astype(jnp.float32)).astype(jnp.bfloat16)


def mul(a, b):
    dot = functools.partial(jnp.dot, preferred_element_type=jnp.float32)
    (ah, al), (bh, bl) = split(a), split(b)
    return dot(ah, bh) + (dot(ah, bl) + dot(al, bh))


def remote(src, dst, send, recv, device):
    return pltpu.make_async_remote_copy(
        src_ref=src, dst_ref=dst, send_sem=send, recv_sem=recv, device_id=device, device_id_type=MESH
    )


class Place:
    def __init__(self, z_size):
        self.row, self.col = lax.axis_index("row"), lax.axis_index("col")
        self.z, self.core, self.z_size = self.row // 2, self.row % 2, z_size
        self.xx, self.yy = self.col // SIDE, self.col % SIDE
        self.up = (2 * ((self.z + 1) % z_size) + self.core, self.col)
        self.down = (2 * ((self.z + z_size - 1) % z_size) + self.core, self.col)
        self.partner = (2 * self.z + 1 - self.core, self.col)

    def side(self, step_x, step_y):
        return (self.row, ((self.xx + step_x) % SIDE) * SIDE + (self.yy + step_y) % SIDE)

    def greet(self):
        barrier = pltpu.get_barrier_semaphore()
        near = (self.up, self.down, self.partner)
        near += (self.side(1, 0), self.side(SIDE - 1, 0), self.side(0, 1), self.side(0, SIDE - 1))
        for device in near:
            pl.semaphore_signal(barrier, inc=1, device_id=device, device_id_type=MESH)
        pl.semaphore_wait(barrier, len(near))


class Ring:
    def __init__(self, place, tops, top_ref, piece_ref, g_ref, sems):
        self.p, self.tops, self.top_ref, self.piece_ref, self.g = place, tops, top_ref, piece_ref, g_ref
        (self.up_s, self.up_r, self.down_s, self.down_r, self.pr_s, self.pr_r,
         self.top_r, self.tu_s, self.td_s, self.tc_s, self.loc) = sems
        self.count, self.height = piece_ref.shape[0], top_ref.shape[0]
        self.chunk = self.height // CHUNKS
        self.ups = place.z_size // 2
        self.downs = place.z_size - 1 - self.ups
        self.total = LAG * self.ups + (CHUNKS if tops else 1)

    def slot(self, z, core):
        at = self.tops * self.height + (2 * (z % self.p.z_size) + core) * self.count
        return self.g.at[pl.ds(pl.multiple_of(at, 8), self.count), :]

    def hop(self, s, way, got=False):
        back = s + 1 if got else s
        if way == "up":
            ref = self.slot(self.p.z + self.p.z_size - back, self.p.core)
            return remote(ref, ref, self.up_s.at[s], self.up_r.at[s], self.p.up)
        ref = self.slot(self.p.z + back, self.p.core)
        return remote(ref, ref, self.down_s.at[s], self.down_r.at[s], self.p.down)

    def share(self, hops, got=False):
        core = 1 - self.p.core if got else self.p.core
        ref = self.slot(self.p.z + self.p.z_size - hops, core)
        return remote(ref, ref, self.pr_s.at[hops], self.pr_r.at[hops], self.p.partner)

    def top_roles(self, b):
        h = (self.p.z + self.p.z_size - b // 2) % self.p.z_size
        hops = jnp.where(h <= self.ups, h, self.p.z_size - h)
        mine = self.p.core == b % 2
        return mine, mine & (h < self.ups), mine & ((h == 0) | (h > self.ups + 1)), mine & (h > 0), hops

    def top_copy(self, b, i, kind):
        ref = self.g.at[pl.ds(pl.multiple_of(b * self.height + i * self.chunk, 8), self.chunk), :]
        send, device = {
            "up": (self.tu_s, self.p.up), "down": (self.td_s, self.p.down), "core": (self.tc_s, self.p.partner)
        }[kind]
        return remote(ref, ref, send.at[b, i], self.top_r.at[b, i], device)

    def place_own(self):
        own = pltpu.make_async_copy(self.piece_ref, self.slot(self.p.z, self.p.core), self.loc.at[0])
        own.start()
        for b in range(self.tops):
            @pl.when(self.p.row == b)
            def _():
                to = self.g.at[pl.ds(b * self.height, self.height), :]
                top = pltpu.make_async_copy(self.top_ref, to, self.loc.at[1])
                top.start()
                top.wait()
        own.wait()

    def begin(self):
        self.hop(0, "up").start()
        self.hop(0, "down").start()
        self.share(0).start()

    def step(self, t):
        for b in range(self.tops):
            mine, to_up, to_down, gets, hops = self.top_roles(b)
            i = t - LAG * hops
            inside = (i >= 0) & (i < CHUNKS)

            @pl.when(inside & gets)
            def _():
                self.top_copy(b, i, "up").wait_recv()

            @pl.when(inside & to_up)
            def _():
                self.top_copy(b, i, "up").start()

            @pl.when(inside & to_down)
            def _():
                self.top_copy(b, i, "down").start()

            @pl.when(inside & mine)
            def _():
                self.top_copy(b, i, "core").start()

        s = t // LAG
        now = (t % LAG == 0) & (s >= 1)

        @pl.when(now & (s <= self.ups))
        def _():
            self.hop(s - 1, "up", True).wait_recv()

            @pl.when(s < self.ups)
            def _():
                self.hop(s, "up").start()

            self.share(s).start()

        @pl.when(now & (s <= self.downs))
        def _():
            self.hop(s - 1, "down", True).wait_recv()

            @pl.when(s < self.downs)
            def _():
                self.hop(s, "down").start()

            self.share(self.p.z_size - s).start()

    def gather(self):
        def rest(s, carry):
            self.share(s, True).wait_recv()
            return carry

        lax.fori_loop(0, self.p.z_size, rest, 0)

        def chunks(i, carry):
            for b in range(self.tops):
                @pl.when(jnp.logical_not(self.top_roles(b)[0]))
                def _():
                    self.top_copy(b, i, "core").wait_recv()

            return carry

        if self.tops:
            lax.fori_loop(0, CHUNKS, chunks, 0)

    def drain(self):
        def hops(way):
            def body(s, carry):
                self.hop(s, way).wait_send()
                return carry

            return body

        def shares(s, carry):
            self.share(s).wait_send()
            return carry

        lax.fori_loop(0, self.ups, hops("up"), 0)
        lax.fori_loop(0, self.downs, hops("down"), 0)
        lax.fori_loop(0, self.p.z_size, shares, 0)

        def chunks(i, carry):
            for b in range(self.tops):
                mine, to_up, to_down, _, _ = self.top_roles(b)
                for role, kind in ((to_up, "up"), (to_down, "down"), (mine, "core")):
                    @pl.when(role)
                    def _():
                        self.top_copy(b, i, kind).wait_send()

            return carry

        if self.tops:
            lax.fori_loop(0, CHUNKS, chunks, 0)


def ring_sems(z_size, tops):
    dma, blocks = pltpu.SemaphoreType.DMA, max(tops, 1)
    return [dma((z_size,))] * 6 + [dma((blocks, CHUNKS))] * 4 + [dma((2,))]


class Torus:
    def __init__(self, place, blocks, x_ref, xo_ref, sems):
        self.p, self.blocks, self.x, self.xo = place, blocks, x_ref, xo_ref
        self.s, self.r, self.loc = sems
        self.half, self.quarter = x_ref.shape[1] // 2, x_ref.shape[1] // 4

    def place_own(self):
        return pltpu.make_async_copy(
            self.x.at[self.blocks], self.xo.at[self.blocks, self.p.xx, self.p.yy], self.loc.at[0]
        )

    def piece(self, k, first, second, part):
        x, y = (first, second) if k == 0 else (second, first)
        start, size = {"all": (0, self.half), "low": (0, self.quarter), "high": (self.quarter, self.quarter)}[part]
        return self.xo.at[
            self.blocks, (self.p.xx + x) % SIDE, (self.p.yy + y) % SIDE, pl.ds(k * self.half + start, size), :
        ]

    def copy(self, k, stage, v, e, receive=False):
        first = (0, SIDE - 1, 1, 2)[v]
        there, part = {0: (0, "all"), 1: (0, "all"), 2: (SIDE - 1, "low"), 3: (1, "high")}[e]
        here = (SIDE - 1, 1, 2, 2)[e]
        step = 1 if e in (0, 2) else SIDE - 1
        device = self.p.side(step, 0) if (k == 0) == (stage == 0) else self.p.side(0, step)
        n = (k * 5 + (0 if stage == 0 else 1 + v)) * 4 + e
        at = here if receive else there
        ref = self.piece(k, at, 0, part) if stage == 0 else self.piece(k, first, at, part)
        src = ref
        if e < 2 and (stage == 0 or v == 0) and not receive:
            src = self.x.at[self.blocks, pl.ds(k * self.half, self.half), :]
        return remote(src, ref, self.s.at[n], self.r.at[n], device)

    def start(self, stage, v, es):
        for e in es:
            for k in range(2):
                self.copy(k, stage, v, e).start()

    def arrive(self, stage, v, e):
        for k in range(2):
            self.copy(k, stage, v, e, True).wait_recv()

    def begin(self):
        self.start(0, 0, (0, 1))
        self.start(1, 0, (0, 1))

    def pass_on(self, stage, v):
        self.arrive(stage, v, 0)
        self.start(stage, v, (2,))
        self.arrive(stage, v, 1)
        self.start(stage, v, (3,))

    def event(self, number):
        if number == 0:
            self.arrive(0, 0, 0)
            self.start(0, 0, (2,))
            self.start(1, 1, (0, 1))
            self.arrive(0, 0, 1)
            self.start(0, 0, (3,))
            self.start(1, 2, (0, 1))
        elif number == 1:
            self.pass_on(1, 0)
        elif number == 2:
            self.arrive(0, 0, 2)
            self.arrive(0, 0, 3)
            self.start(1, 3, (0, 1))
        elif number < 6:
            self.pass_on(1, number - 2)

    def complete(self, v):
        self.arrive(1, v, 2)
        self.arrive(1, v, 3)

    def drain(self):
        for k in range(2):
            for e in range(4):
                self.copy(k, 0, 0, e).wait_send()
                for v in range(4):
                    self.copy(k, 1, v, e).wait_send()


def torus_sems():
    return [pltpu.SemaphoreType.DMA((40,))] * 2 + [pltpu.SemaphoreType.DMA((1,))]


def run(begin, end, *steps):
    def body(t, carry):
        for step in steps:
            step(t)
        return carry

    lax.fori_loop(begin, end, body, 0)


def plain_kernel(z_size, piece_ref, x_ref, g_ref, xo_ref, *sems):
    place = Place(z_size)
    place.greet()
    ring = Ring(place, 0, piece_ref, piece_ref, g_ref, sems[:11])
    torus = Torus(place, pl.ds(0, x_ref.shape[0]), x_ref, xo_ref, sems[11:])
    own = torus.place_own()
    own.start()
    torus.begin()
    ring.place_own()
    ring.begin()
    own.wait()
    run(0, ring.total, ring.step)
    for number in range(6):
        torus.event(number)
    for v in range(4):
        torus.complete(v)
    ring.gather()
    ring.drain()
    torus.drain()


def exchange(piece, x, owners, ident):
    vmem, hbm = pl.BlockSpec(memory_space=pltpu.VMEM), pl.BlockSpec(memory_space=pl.ANY)
    g, xo = pl.pallas_call(
        functools.partial(plain_kernel, owners // 2),
        out_shape=(
            jax.ShapeDtypeStruct((owners * piece.shape[0], piece.shape[1]), jnp.float32),
            jax.ShapeDtypeStruct((x.shape[0], SIDE, SIDE) + x.shape[1:], jnp.float32),
        ),
        in_specs=[vmem, vmem],
        out_specs=(hbm, hbm),
        scratch_shapes=ring_sems(owners // 2, 0) + torus_sems(),
        compiler_params=pltpu.CompilerParams(collective_id=ident, has_side_effects=True),
    )(piece, x)
    return g, xo.reshape(x.shape[0], SIDE * SIDE * x.shape[1], x.shape[2])


def packed_kernel(ticks, z_size, index_ref, take_ref, stop_ref, x_ref, full_ref, f_ref, t_ref,
                  ptop_ref, ppiece_ref, spiece_ref, gs_ref, gp_ref, rows_ref, y_ref, sh_s, sh_r, *sems):
    place = Place(z_size)
    spare = jnp.zeros((ptop_ref.shape[1] - ticks * x_ref.shape[1], x_ref.shape[2]), jnp.float32)
    ptop_ref[...] = jnp.concatenate([x_ref[k] for k in range(ticks)] + [spare], axis=0).T
    first = rows_ref.shape[0]

    def pack(i, carry):
        for n in range(8):
            at = i * 8 + n
            row = index_ref[first + at]
            ppiece_ref[pl.ds(at, 1), :] = ptop_ref[pl.ds(row, 1), :]
            spiece_ref[pl.ds(at, 1), :] = stop_ref[pl.ds(row, 1), :]
        return carry

    lax.fori_loop(0, ppiece_ref.shape[0] // 8, pack, 0)
    place.greet()
    panel = Ring(place, ticks, ptop_ref, ppiece_ref, gp_ref, sems[:11])
    slab = Ring(place, ticks, stop_ref, spiece_ref, gs_ref, sems[11:22])
    torus = Torus(place, pl.ds(0, ticks), x_ref, full_ref, sems[22:25])
    mine = (ticks + 1) * place.core
    corner = Torus(place, pl.ds(mine, ticks + 1), y_ref, f_ref, sems[25:])
    depth, width = y_ref.shape[1:]

    own = torus.place_own()
    own.start()
    torus.begin()
    panel.place_own()
    panel.begin()
    slab.place_own()
    own.wait()
    total = panel.total
    shift = total - SPREAD
    begin = 0
    for number in range(7):
        end = total if number == 6 else 2 + (total - 2) * number // 6
        for low, high, both in ((begin, min(end, shift), False), (max(begin, shift), end, True)):
            if low < high:
                if both and low == shift:
                    slab.begin()
                steps = (panel.step,) + ((lambda t: slab.step(t - shift),) if both else ())
                run(low, high, *steps)
        begin = end
        torus.event(number)
    panel.gather()

    def load(i, carry):
        for n in range(8):
            at = i * 8 + n
            rows_ref[pl.ds(at, 1), :] = gp_ref[pl.ds(index_ref[at], 1), :]
        return carry

    def turn(ref, n, k):
        return ref[pl.ds(n * width, width), :].T[k * depth:(k + 1) * depth]

    @pl.when(place.core == 0)
    def _():
        lax.fori_loop(0, width // 8, load, 0)
        y_ref[DIAGONAL[0]] = turn(gp_ref, 0, 0)
        y_ref[DIAGONAL[1]] = turn(gp_ref, 1, 1)
        y_ref[ACROSS[0]] = turn(rows_ref, 0, 0)

    @pl.when(place.core == 1)
    def _():
        lax.fori_loop(width // 8, 3 * width // 8, load, 0)
        y_ref[DIAGONAL[2]] = turn(gp_ref, 2, 2)
        y_ref[ACROSS[1]] = turn(rows_ref, 1, 0)
        y_ref[ACROSS[2]] = turn(rows_ref, 2, 1)

    lax.fori_loop(3 * width // 8, rows_ref.shape[0] // 8, load, 0)
    patches = rows_ref[pl.ds(3 * width, 2 * PATCH), :].T
    zeros = jnp.zeros((depth, width - 2 * PATCH), jnp.float32)
    y_ref[mine + ticks] = jnp.concatenate([patches[:depth, :PATCH], patches[depth:2 * depth, PATCH:], zeros], axis=1)

    run(total, total + 2, lambda t: slab.step(t - shift))
    own = corner.place_own()
    own.start()
    corner.begin()
    own.wait()
    begin, last = total + 2, total + shift

    def pass_share(k, v, receive=False):
        first = (0, SIDE - 1, 1, 2)[v]
        to = pl.ds((ticks + 1) * (1 - place.core if receive else place.core), ticks)
        half = pl.ds(k * corner.half, corner.half)
        if k == 0:
            ref = f_ref.at[to, (place.xx + first) % SIDE, :, half, :]
        else:
            ref = f_ref.at[to, :, (place.yy + first) % SIDE, half, :]
        return remote(ref, ref, sh_s.at[k, v], sh_r.at[k, v], place.partner)

    def pick(i, carry):
        for n in range(8):
            at = i * 8 + n
            t_ref[pl.ds(at, 1), :] = gs_ref[pl.ds(take_ref[at], 1), :]
        return carry

    for number in range(7):
        end = last if number == 6 else begin + (last - begin) // (7 - number)
        if begin < end:
            run(begin, end, lambda t: slab.step(t - shift))
        begin = end
        corner.event(number)
        if number == 6:
            slab.gather()
            lax.fori_loop(0, t_ref.shape[0] // 8, pick, 0)
        if number >= 4:
            v = number - 4
            corner.complete(v)
            for k in range(2):
                pass_share(k, v).start()
    corner.complete(3)
    for k in range(2):
        pass_share(k, 3).start()
    for v in range(4):
        torus.complete(v)
    for v in range(4):
        for k in range(2):
            pass_share(k, v, True).wait_recv()
            pass_share(k, v).wait_send()
    panel.drain()
    slab.drain()
    torus.drain()
    corner.drain()


def packed_exchange(index, take, slab, x, ticks, owners, ident):
    vmem, smem = pl.BlockSpec(memory_space=pltpu.VMEM), pl.BlockSpec(memory_space=pltpu.SMEM)
    z_size, blocks = owners // 2, 2 * (ticks + 1)
    rows, cols = slab.shape
    packed = ticks * rows + owners * SLOTS
    torus = (SIDE, SIDE) + x.shape[1:]
    f32 = jnp.float32
    full, f, t = pl.pallas_call(
        functools.partial(packed_kernel, ticks, z_size),
        out_shape=(
            jax.ShapeDtypeStruct((ticks,) + torus, f32),
            jax.ShapeDtypeStruct((blocks,) + torus, f32),
            jax.ShapeDtypeStruct((take.shape[0], cols), f32),
        ),
        in_specs=[smem, smem, vmem, vmem],
        out_specs=(vmem, vmem, vmem),
        scratch_shapes=[
            pltpu.VMEM((rows, TILE), f32),
            pltpu.VMEM((SLOTS, TILE), f32),
            pltpu.VMEM((SLOTS, cols), f32),
            pltpu.VMEM((packed, cols), f32),
            pltpu.VMEM((packed, TILE), f32),
            pltpu.VMEM((index.shape[0] - SLOTS, TILE), f32),
            pltpu.VMEM((blocks,) + x.shape[1:], f32),
            pltpu.SemaphoreType.DMA((2, 4)), pltpu.SemaphoreType.DMA((2, 4)),
        ] + ring_sems(z_size, ticks) * 2 + torus_sems() * 2,
        compiler_params=pltpu.CompilerParams(collective_id=ident, has_side_effects=True),
    )(index, take, slab, x)
    width, depth = x.shape[2], SIDE * SIDE * x.shape[1]
    return full.reshape(ticks, depth, width), f.reshape(blocks, depth, width), t


def invert_tiles(tiles):
    k = lax.broadcasted_iota(jnp.int32, tiles[0].shape, 0)
    r = lax.broadcasted_iota(jnp.int32, tiles[0].shape, 1)
    eye = jnp.where(k == r, 1.0, 0.0).astype(jnp.float32)
    strict = [jnp.where(k < r, tile, 0.0) for tile in tiles]
    power = [jnp.where(k // 16 == r // 16, -tile, 0.0) for tile in strict]
    inverse = [eye + tile for tile in power]
    for _ in range(3):
        power = [mul(tile, tile) for tile in power]
        inverse = [one + mul(one, tile) for one, tile in zip(inverse, power)]
    for size in (16, 32, 64):
        pick = (k // (2 * size) == r // (2 * size)) & (k // size != r // size)
        half = [mul(jnp.where(pick, tile, 0.0), one) for tile, one in zip(strict, inverse)]
        inverse = [one - mul(one, tile) for one, tile in zip(inverse, half)]
    return inverse


def finish_kernel(ticks, together, f_ref, full_ref, t_ref, base_ref, ints_ref, place_ref, moved_ref,
                  out_ref, inv_ref, u_ref):
    width = f_ref.shape[1]
    tiles = width // TILE
    inv_ref[...] = jnp.zeros_like(inv_ref)

    def invert(bs):
        spots = [(b, pl.ds(j * TILE, TILE)) for b in bs for j in range(tiles)]
        inverses = invert_tiles([f_ref[b + 2 * (b // 2), spot, spot] for b, spot in spots])
        for (b, spot), one in zip(spots, inverses):
            inv_ref[b, spot, spot] = one

    if together:
        invert(range(ticks))
    else:
        run(0, ticks, lambda b: invert([b]))
    size = TILE
    while size < width:
        spots = [
            (b, pl.ds(low, size), pl.ds(low + size, size))
            for b in range(ticks) for low in range(0, width, 2 * size)
        ]
        half = [mul(f_ref[DIAGONAL[b], near, far], inv_ref[b, far, far]) for b, near, far in spots]
        for (b, near, far), tile in zip(spots, half):
            inv_ref[b, near, far] = -mul(inv_ref[b, near, near], tile)
        size *= 2

    off = 0
    for b in range(ticks):
        rhs = t_ref[pl.ds(b * width, width), :].T
        for j in range(b):
            rhs = rhs - mul(u_ref[j], f_ref[ACROSS[off]])
            off += 1
        u_ref[b] = mul(rhs, inv_ref[b])

    me = ints_ref[PATCH]

    @pl.when(me < ticks)
    def _():
        out_ref[...] = u_ref[jnp.minimum(me, ticks - 1)].T

    @pl.when(me >= ticks)
    def _():
        out_ref[...] = base_ref[...]

        def place_row(s, carry):
            to = ints_ref[s]

            @pl.when(to >= 0)
            def _():
                out_ref[pl.ds(to, 1), :] = t_ref[pl.ds(ticks * width + s, 1), :]

            return carry

        lax.fori_loop(0, PATCH, place_row, 0)
        s = lax.broadcasted_iota(jnp.int32, (PATCH, place_ref.shape[1]), 0)
        pick = jnp.where(place_ref[0:1, :] == s, 1.0, 0.0).astype(jnp.bfloat16)
        total = None
        for k in range(ticks):
            left = full_ref[k]
            if k < ticks - 1:
                high, low = split(f_ref[ticks + (ticks + 1) * (me % 2), :, pl.ds(k * PATCH, PATCH)])
                new = jnp.dot(high, pick, preferred_element_type=jnp.float32)
                new = new + jnp.dot(low, pick, preferred_element_type=jnp.float32)
                left = jnp.where(moved_ref[k:k + 1, :] > 0, new, left)
            part = mul(u_ref[k], left)
            total = part if total is None else total + part
        out_ref[...] = out_ref[...] - total.T


def finish(ticks, together, factor, full, t, base, ints, place, moved):
    vmem = pl.BlockSpec(memory_space=pltpu.VMEM)
    width, cols = factor.shape[1], t.shape[1]
    return pl.pallas_call(
        functools.partial(finish_kernel, ticks, together),
        out_shape=jax.ShapeDtypeStruct(base.shape, jnp.float32),
        in_specs=[vmem] * 4 + [pl.BlockSpec(memory_space=pltpu.SMEM), vmem, vmem],
        out_specs=vmem,
        scratch_shapes=[
            pltpu.VMEM((ticks, width, width), jnp.float32), pltpu.VMEM((ticks, cols, width), jnp.float32)
        ],
        compiler_params=pltpu.CompilerParams(vmem_limit_bytes=50 * 1024 * 1024),
    )(factor, full, t, base, ints, place, moved)


def find(a, b, base):
    i = jnp.arange(b.shape[0], dtype=jnp.int32)
    return jnp.max(jnp.where(a[:, None] == b[None, :], base + i[None, :], -1), axis=1)


def packing(pivots, rows):
    src = pivots.reshape(-1)
    owner = src // rows
    e = jnp.arange(src.shape[0], dtype=jnp.int32)
    same = (owner[:, None] == owner[None, :]) & (e[None, :] < e[:, None])
    return src, owner, jnp.sum(same.astype(jnp.int32), axis=1)


def rows_of(array, index):
    return jnp.take(array, index, axis=0, mode="clip")


def update(packed, owners, slab, panels, pivots, packs):
    rows, cols = slab.shape
    ticks, width = pivots.shape
    depth = panels.shape[2]
    me = lax.axis_index("row")
    src, owner, rank = packs
    top = ticks * width
    g = src
    if packed:
        g = jnp.where(owner < ticks, src, top + jnp.minimum(owner * SLOTS + rank, owners * SLOTS - 1))
        s = jnp.arange(SLOTS, dtype=jnp.int32)
        held = (owner[None, :] == me) & (rank[None, :] == s[:, None])
        listed = jnp.max(jnp.where(held, src[None, :] - me * rows, 0), axis=1)
    x_panels = jnp.transpose(panels, (0, 2, 1))

    s0, s1, s2 = pivots
    g0, g1, g2 = g[:width], g[width:2 * width], g[2 * width:]
    back = find(s2, s1, width)
    f2 = find(jnp.where(back >= 0, back, s2), s0, 0)
    f1 = find(s1, s0, 0)
    row20 = jnp.where(back >= 0, back, g2)
    take_t = jnp.concatenate([g0, jnp.where(f1 >= 0, f1, g1), jnp.where(f2 >= 0, f2, row20)])
    mine = me * rows + jnp.arange(rows, dtype=jnp.int32)
    h2 = find(mine, s2, 2 * width)
    pos1 = jnp.where(h2 >= 0, h2, mine)
    h1 = find(pos1, s1, width)
    pos0 = jnp.where(h1 >= 0, h1, pos1)
    h0 = find(pos0, s0, 0)
    orig = jnp.where(h0 >= 0, h0, pos0)
    moved0, moved1 = pos0 != mine, pos1 != mine
    touched = orig != mine
    q = jnp.arange(rows, dtype=jnp.int32)
    if packed:
        place = jnp.sum(((q[None, :] < q[:, None]) & touched[None, :]).astype(jnp.int32), axis=1)
        place = jnp.where(touched, place, -1)
        s = jnp.arange(PATCH, dtype=jnp.int32)
        pick = place[None, :] == s[:, None]
        to = jnp.max(jnp.where(pick, q[None, :], -1), axis=1)
        from0 = jnp.max(jnp.where(pick & moved0[None, :], pos0[None, :], 0), axis=1)
        from1 = jnp.max(jnp.where(pick & moved1[None, :], pos1[None, :], 0), axis=1)
        from_slab = jnp.max(jnp.where(pick, orig[None, :], 0), axis=1)
    else:
        from0, from1 = pos0, pos1

    if packed:
        index = jnp.concatenate([g1, row20, g2, from0, from1, listed])
        take = jnp.concatenate([take_t, from_slab])
        full, factor, t = packed_exchange(index, take, slab, x_panels, ticks, owners, 0)
        base = slab
        moved = jnp.stack([moved0, moved1] + [touched] * 6).astype(jnp.int32)
    else:
        panel_rows = jnp.concatenate(
            [panels[k] for k in range(ticks)] + [jnp.zeros((rows, 128 - ticks * depth), jnp.float32)], axis=1
        )
        g_panel, full = exchange(panel_rows, x_panels, owners, 1)

        def block(index, k):
            return rows_of(g_panel, index)[:, k * depth:(k + 1) * depth].T

        lower = [g_panel[k * width:(k + 1) * width, k * depth:(k + 1) * depth].T for k in range(ticks)]
        corner = [lower[0], lower[1], block(g1, 0), block(from0, 0)]
        corner += [lower[2], block(row20, 0), block(g2, 1), block(from1, 1)]
        g_slab, factor = exchange(slab, jnp.stack(corner), owners, 2)
        base = jnp.where(touched[:, None], rows_of(g_slab, orig), slab)
        full = jnp.stack([
            jnp.where(moved0[None, :], factor[ticks], full[0]),
            jnp.where(moved1[None, :], factor[2 * ticks + 1], full[1]),
            full[2],
        ])
        moved = jnp.zeros((8, rows), jnp.int32)
        place, to = jnp.full((rows,), -1, jnp.int32), jnp.full((PATCH,), -1, jnp.int32)
        t = rows_of(g_slab, jnp.concatenate([take_t, jnp.zeros((PATCH,), jnp.int32)]))
    ints = jnp.concatenate([to, jnp.full((8,), me, jnp.int32)])
    place = jnp.broadcast_to(place[None, :], (8, rows))
    return factor, full, t, base, ints, place, moved


def solution(mesh):
    owners = mesh.shape["row"]

    def local(slab, panels, pivots):
        rows, ticks = slab.shape[0], pivots.shape[0]
        packs = packing(pivots, rows)
        _, owner, rank = packs
        fits = jnp.all((owner < ticks) | (rank < SLOTS))
        ready = update(True, owners, slab, panels, pivots, packs)
        return lax.cond(
            fits,
            lambda ready, rest: finish(ticks, True, *ready),
            lambda ready, rest: finish(ticks, False, *update(False, owners, *rest)),
            ready, (slab, panels, pivots, packs),
        )

    in_specs = (P("row", "col"), P(None, "row", "col"), P())
    return jax.shard_map(local, mesh=mesh, in_specs=in_specs, out_specs=P("row", "col"), check_vma=False)
```
